32 devices in a mesh: grp: 4 (over y, x), dev: 8 (over z, core).
Axes of the slice: x: 2, y: 2, z: 4, core: 2. Of those that a mesh axis runs over, the one named last changes fastest.
Arguments:
- schur: bfloat16 [32, 1024, 1024], P(('grp', 'dev'))
- omega: bfloat16 [32, 1024, 512], P(('grp', 'dev'))
- face_rows: int32 [32, 4, 128], P(('grp', 'dev')), may hold values from 0 to 1023, as said below
Outputs:
- basis: bfloat16 [32, 1024, 512], P(('grp', 'dev'))
- factor: float32 [512, 512], P('dev')
The draws below stay inside these ranges and needn't reach their ends.
Inputs may be any that keep to these rules, and one draw needn't show every extreme that they name: `face_rows`: the 512 rows of one subdomain are distinct.
All inputs are finite; a program needn't handle non-finite values.
Results may differ from the reference program's by a relative error of at most 0.0095.
Values may be sent and summed in bfloat16 or wider, within the bound.
No kernel may reach another device: no remote copies, remote signals or barrier semaphores. Data moves between devices by JAX's collectives and lax.ppermute only.
A program may use at most 64 MiB of HBM per device.

```python
import math
import jax
import jax.numpy as jnp
from jax import lax

NS = 1024
K = 512
FR = 128
SUBS = 32
N_GRP = 4
N_DEV = 8


def draw_schur(key, part):
    first_key, second_key = jax.random.split(jax.random.fold_in(key, 11))
    noise = jax.random.normal(first_key, (SUBS, NS, NS), jnp.float32)
    diagonal = jnp.exp(jax.random.uniform(second_key, (SUBS, NS), jnp.float32, 0.0, math.log(2.0)))
    identity = jnp.eye(NS, dtype=jnp.float32)
    return (noise * (0.3 / math.sqrt(NS)) + identity[None, :, :] * diagonal[:, :, None]).astype(jnp.bfloat16)


def draw_omega(key, part):
    first_key, second_key = jax.random.split(jax.random.fold_in(key, 23))
    pair_key = jax.random.fold_in(key, 59)
    base = jax.random.normal(first_key, (SUBS, NS, K), jnp.float32)
    shared = jax.random.normal(second_key, (SUBS, NS, K // 8), jnp.float32)
    paired = jax.random.permutation(pair_key, SUBS) % K
    marked = (paired[:, None] == jnp.arange(K)[None, :]).astype(jnp.float32)
    boost = 1.0 + 15.0 * marked
    return ((base + 0.8 * jnp.repeat(shared, 8, axis=-1)) * boost[:, None, :]).astype(jnp.bfloat16)


def draw_face_rows(key, part):
    keys = jax.random.split(jax.random.fold_in(key, 37), SUBS)
    orders = jax.vmap(lambda k: jax.random.permutation(k, NS))(keys)
    return orders[:, :4 * FR].reshape(SUBS, 4, FR).astype(jnp.int32)


def setup_inputs(seed: int = 0) -> dict:
    key_list = jax.random.split(jax.random.key(seed), 4)
    return {
        "schur": draw_schur(jax.random.fold_in(key_list[3], 71), 0),
        "omega": draw_omega(jax.random.fold_in(key_list[3], 71), 0),
        "face_rows": draw_face_rows(jax.random.fold_in(key_list[3], 71), 0),
    }


def local_product(pair):
    return jnp.dot(pair[0].astype(jnp.float32), pair[1].astype(jnp.float32), preferred_element_type=jnp.float32).astype(jnp.bfloat16)

def assemble(block, face_rows):
    width = block.shape[-1]
    faces = jax.vmap(lambda a, i: jnp.take(a, i.reshape(-1), axis=0))(block, face_rows)
    faces = faces.reshape(N_GRP, N_DEV, 4, FR, width)
    recv0 = jnp.roll(faces[:, :, 1], 1, axis=1)
    recv1 = jnp.roll(faces[:, :, 0], -1, axis=1)
    recv2 = jnp.roll(faces[:, :, 3], 1, axis=0)
    recv3 = jnp.roll(faces[:, :, 2], -1, axis=0)
    received = jnp.stack([recv0, recv1, recv2, recv3], axis=2).reshape(SUBS, 4 * FR, width)

    def add_one(a, i, r):
        return a.astype(jnp.float32).at[i.reshape(-1)].add(r.astype(jnp.float32))
    return jax.vmap(add_one)(block, face_rows, received)

def reference(schur, omega, face_rows):
    first = lax.map(local_product, (schur, omega))
    spread = assemble(first, face_rows).astype(jnp.bfloat16)
    second = lax.map(local_product, (schur, spread))
    summed = assemble(second, face_rows)

    def weights(i):
        return jnp.ones((NS,), jnp.float32).at[i.reshape(-1)].set(jnp.float32(1.0 / math.sqrt(2.0)))
    tall = summed * jax.vmap(weights)(face_rows)[:, :, None]

    def add_gram(total, piece):
        return (total + jnp.dot(piece.T, piece, precision=lax.Precision.HIGHEST), None)
    gram, unused = lax.scan(add_gram, jnp.zeros((K, K), jnp.float32), tall)
    gram = gram / (SUBS * NS)
    lower = jnp.linalg.cholesky(gram)

    def solve_one(piece):
        return jax.scipy.linalg.solve_triangular(lower, piece.T, lower=True).T.astype(jnp.bfloat16)
    basis = lax.map(solve_one, tall)
    return (basis, lower.T)
```

```python
import functools
import math

import jax
import jax.numpy as jnp
from jax import lax
from jax.experimental import pallas as pl
from jax.experimental.pallas import tpu as pltpu
from jax.sharding import PartitionSpec as P

F32 = jnp.float32
BF16 = jnp.bfloat16
BLOCK = 128
AXES = ("grp", "dev")
VMEM = pl.BlockSpec(memory_space=pltpu.VMEM)


def slots_of(face_ref):
    rows = face_ref[...]
    odd_d = lax.rem(lax.axis_index("dev"), 2) == 1
    odd_g = lax.rem(lax.axis_index("grp"), 2) == 1
    f0, f1, f2, f3 = (rows[i : i + 1, :] for i in range(4))
    return (
        jnp.where(odd_d, f0, f1),
        jnp.where(odd_d, f1, f0),
        jnp.where(odd_g, f2, f3),
        jnp.where(odd_g, f3, f2),
    )


def gather_matrix(slots, columns, start):
    out = []
    for slot in slots:
        count = slot.shape[1]
        column = jnp.transpose(jnp.broadcast_to(slot.astype(F32), (8, count)))[:, 0:1]
        lanes = lax.broadcasted_iota(jnp.int32, (count, columns), 1) + start
        out.append((column == lanes.astype(F32)).astype(BF16))
    return jnp.concatenate(out, axis=0)


def scatter_matrix(slots, rows):
    out = []
    for slot in slots:
        sub = lax.broadcasted_iota(jnp.int32, (rows, slot.shape[1]), 0)
        out.append((sub == slot).astype(F32).astype(BF16))
    return jnp.concatenate(out, axis=1)


def dot(a, b):
    return jnp.dot(a, b, preferred_element_type=F32)


def contract(a, b, dims, exact=False):
    return lax.dot_general(
        a,
        b,
        (dims, ((), ())),
        precision=lax.Precision.HIGHEST if exact else None,
        preferred_element_type=F32,
    )


def emit_faces(step, steps, total, value, face_ref, face_outs):
    rows = value.shape[0]
    picked = dot(gather_matrix(slots_of(face_ref), rows, step * rows), value)

    @pl.when(step == 0)
    def _():
        total[...] = picked

    @pl.when(step > 0)
    def _():
        total[...] += picked

    @pl.when(step == steps - 1)
    def _():
        count = face_outs[0].shape[0]
        for i, out in enumerate(face_outs):
            out[...] = total[pl.ds(i * count, count), :].astype(BF16)


def first_kernel(steps, schur_ref, omega_ref, face_ref, first_ref, f0, f1, f2, f3, total):
    step = pl.program_id(0)
    value = dot(schur_ref[...], omega_ref[...]).astype(BF16)
    first_ref[...] = value
    emit_faces(step, steps, total, value, face_ref, (f0, f1, f2, f3))


def second_kernel(
    steps, schur_ref, first_ref, face_ref, r0, r1, r2, r3, second_ref, f0, f1, f2, f3, total, spread
):
    step = pl.program_id(0)

    @pl.when(step == 0)
    def _():
        received = jnp.concatenate([r[...] for r in (r0, r1, r2, r3)], axis=0)
        place = scatter_matrix(slots_of(face_ref), first_ref.shape[0])
        spread[...] = (first_ref[...].astype(F32) + dot(place, received)).astype(BF16)

    value = dot(schur_ref[...], spread[...]).astype(BF16)
    second_ref[...] = value
    emit_faces(step, steps, total, value, face_ref, (f0, f1, f2, f3))


def apply_schur(kernel, matrix, whole, faces, extra, scratch):
    rows, inner = matrix.shape
    columns = whole.shape[1]
    count = faces.shape[1]
    steps = 4 if rows % (4 * BLOCK) == 0 else 1
    chunk = rows // steps
    full = lambda shape: pl.BlockSpec(shape, lambda i: (0,) * len(shape))
    face_out = jax.ShapeDtypeStruct((count, columns), BF16)
    return pl.pallas_call(
        functools.partial(kernel, steps),
        grid=(steps,),
        in_specs=[
            pl.BlockSpec((chunk, inner), lambda i: (i, 0)),
            full(whole.shape),
            full(faces.shape),
        ]
        + [full(x.shape) for x in extra],
        out_specs=[pl.BlockSpec((chunk, columns), lambda i: (i, 0))]
        + [full((count, columns))] * 4,
        out_shape=[jax.ShapeDtypeStruct((rows, columns), BF16)] + [face_out] * 4,
        scratch_shapes=[pltpu.VMEM((4 * count, columns), F32)] + scratch,
    )(matrix, whole, faces, *extra)


def triangle(count):
    return [(i, j) for i in range(count) for j in range(i, count)]


def gram_kernel(second_ref, face_ref, r0, r1, r2, r3, tall_ref, keep_ref, send_ref, packed):
    received = jnp.concatenate([r[...] for r in (r0, r1, r2, r3)], axis=0)
    rows, columns = second_ref.shape
    place = scatter_matrix(slots_of(face_ref), rows)
    shared = dot(place, jnp.ones((place.shape[1], BLOCK), BF16))
    weight = jnp.where(shared > 0.5, F32(1.0 / math.sqrt(2.0)), F32(1.0))
    weight = jnp.concatenate([weight] * (columns // BLOCK), axis=1)
    tall = ((second_ref[...].astype(F32) + dot(place, received)) * weight).astype(BF16)
    tall_ref[...] = tall
    side = jnp.transpose(tall)
    blocks = columns // BLOCK
    at = 0
    for i in range(blocks):
        strip = dot(side[i * BLOCK : (i + 1) * BLOCK, :], tall[:, i * BLOCK :])
        for j in range(i, blocks):
            packed[pl.ds(at * BLOCK, BLOCK), :] = strip[:, (j - i) * BLOCK : (j - i + 1) * BLOCK]
            at += 1
    half = keep_ref.shape[0]
    filled = at * BLOCK
    if packed.shape[0] > filled:
        packed[pl.ds(filled, packed.shape[0] - filled), :] = jnp.zeros(
            (packed.shape[0] - filled, BLOCK), F32
        )
    core = lax.rem(lax.axis_index("dev"), 2)
    keep_ref[...] = packed[pl.ds(pl.multiple_of(core * half, 8), half), :]
    send_ref[...] = packed[pl.ds(pl.multiple_of((1 - core) * half, 8), half), :].astype(send_ref.dtype)


def partner(index, step, count):
    if count & (count - 1) == 0:
        return index ^ step
    return lax.rem(index + count - step, count) if not isinstance(index, int) else (index - step) % count


def target(index, step, count):
    if count & (count - 1) == 0:
        return index ^ step
    return lax.rem(index + step, count) if not isinstance(index, int) else (index + step) % count


def split_kernel(count, keep_ref, got_ref, own_ref, *rest):
    outs, total = rest[:-1], rest[-1]
    total[...] = keep_ref[...] + got_ref[...].astype(F32)
    me = lax.axis_index("grp")
    size = own_ref.shape[0]
    own_ref[...] = total[pl.ds(pl.multiple_of(me * size, 8), size), :]
    for step, out in enumerate(outs, 1):
        to = target(me, step, count)
        out[...] = total[pl.ds(pl.multiple_of(to * size, 8), size), :].astype(out.dtype)


def add_kernel(*refs):
    total = refs[0][...]
    for ref in refs[1:-1]:
        total = total + ref[...].astype(F32)
    refs[-1][...] = total.astype(refs[-1].dtype)


def ordered_kernel(count, own_ref, *rest):
    got, out_ref, table = rest[:-2], rest[-2], rest[-1]
    me = lax.axis_index("dev") // 2
    size = own_ref.shape[0]

    def put(index, value):
        table[pl.ds(pl.multiple_of(index * size, 8), size), :] = value.astype(F32)

    put(me, own_ref[...])
    for step, ref in enumerate(got, 1):
        put(partner(me, step, count), ref[...])
    total = table[pl.ds(0, size), :]
    for i in range(1, count):
        total = total + table[pl.ds(i * size, size), :]
    out_ref[...] = total.astype(out_ref.dtype)


def join_kernel(count, own_ref, *rest):
    got, out_ref = rest[:-1], rest[-1]
    me = lax.axis_index("grp")
    size = own_ref.shape[0]
    out_ref[pl.ds(pl.multiple_of(me * size, 8), size), :] = own_ref[...]
    for step, ref in enumerate(got, 1):
        out_ref[pl.ds(pl.multiple_of(partner(me, step, count) * size, 8), size), :] = ref[...]


def call(kernel, args, outs, scratch=()):
    return pl.pallas_call(
        kernel,
        in_specs=[VMEM] * len(args),
        out_specs=[VMEM] * len(outs),
        out_shape=[jax.ShapeDtypeStruct(s, t) for s, t in outs],
        scratch_shapes=[pltpu.VMEM(s, t) for s, t in scratch],
    )(*args)


def eliminate(block, put_upper, put_inverse):
    size = block.shape[0]
    row = lax.broadcasted_iota(jnp.int32, (size, size), 0)
    column = lax.broadcasted_iota(jnp.int32, (size, size), 1)
    unit = (row == column).astype(F32)
    for start in range(0, size, 8):
        left = block.shape[0]
        panel = [
            jnp.broadcast_to(block[:, start + j : start + j + 1], (left, size)) for j in range(8)
        ]
        for j in range(8):
            scale = lax.rsqrt(panel[j][j : j + 1, :])
            upper = block[j : j + 1, :] * scale
            inverse = unit[j : j + 1, :] * scale
            lower = panel[j] * scale
            put_upper(start + j, upper)
            put_inverse(start + j, inverse)
            block = block - lower * upper
            unit = unit - lower * inverse
            for i in range(j + 1, 8):
                panel[i] = panel[i] - lower * (panel[i][j : j + 1, :] * scale)
        block = block[8:]
        unit = unit[8:]


def factor_kernel(total_rows, own_ref, other_ref, tall_ref, basis_ref, factor_ref, packed, upper, inverse):
    half = own_ref.shape[0]
    core = lax.rem(lax.axis_index("dev"), 2)
    packed[pl.ds(pl.multiple_of(core * half, 8), half), :] = own_ref[...].astype(F32)
    packed[pl.ds(pl.multiple_of((1 - core) * half, 8), half), :] = other_ref[...].astype(F32)
    columns = tall_ref.shape[1]
    blocks = columns // BLOCK
    span = lambda i: pl.ds(i * BLOCK, BLOCK)
    gram = {
        pair: packed[span(at), :] * F32(1.0 / total_rows) for at, pair in enumerate(triangle(blocks))
    }
    row = lax.broadcasted_iota(jnp.int32, (BLOCK, BLOCK), 0)
    column = lax.broadcasted_iota(jnp.int32, (BLOCK, BLOCK), 1)
    upper[...] = jnp.zeros(upper.shape, F32)
    inverse[...] = jnp.zeros(inverse.shape, F32)
    for b in range(blocks):

        def put_upper(i, value):
            upper[pl.ds(b * BLOCK + i, 1), b * BLOCK : (b + 1) * BLOCK] = value

        def put_inverse(i, value):
            inverse[pl.ds(b * BLOCK + i, 1), b * BLOCK : (b + 1) * BLOCK] = value

        eliminate(gram[b, b], put_upper, put_inverse)
        here = slice(b * BLOCK, (b + 1) * BLOCK)
        upper[here, here] = jnp.where(row <= column, upper[here, here], F32(0.0))
        diagonal = jnp.where(row >= column, inverse[here, here], F32(0.0))
        strip = {}
        for j in range(b + 1, blocks):
            strip[j] = contract(diagonal, gram[b, j], ((1,), (0,)), exact=True)
            upper[here, j * BLOCK : (j + 1) * BLOCK] = strip[j]
        for i in range(b + 1, blocks):
            for j in range(i, blocks):
                gram[i, j] = gram[i, j] - contract(strip[i], strip[j], ((0,), (0,)), exact=True)
        inverse[here, here] = diagonal
        if b:
            before = slice(0, b * BLOCK)
            mixed = contract(upper[before, here], inverse[before, before], ((0,), (0,)), exact=True)
            inverse[here, before] = -contract(diagonal, mixed, ((1,), (0,)), exact=True)
        reach = slice(0, (b + 1) * BLOCK)
        basis_ref[:, here] = contract(
            tall_ref[:, reach], inverse[here, reach].astype(BF16), ((1,), (1,))
        ).astype(BF16)
    share = factor_ref.shape[0]
    factor_ref[...] = upper[pl.ds(pl.multiple_of(lax.axis_index("dev") * share, 8), share), :]


def per_device(schur, omega, face_rows):
    matrix, tests, faces = schur[0], omega[0], face_rows[0]
    groups = lax.axis_size("grp")
    devs = lax.axis_size("dev")
    depth = devs // 2
    rows, columns = tests.shape

    def flat(pairs):
        return [(g * devs + d, h * devs + e) for g, d, h, e in pairs]

    everywhere = [(g, d) for g in range(groups) for d in range(devs)]
    twin = flat([(g, d, g, d ^ 1) for g, d in everywhere])
    along_dev = flat([(g, d, g, (d + 1 if d % 2 else d - 1) % devs) for g, d in everywhere])
    pair_grp = flat([(g, d, g ^ 1, d) for g, d in everywhere])
    along_grp = flat([(g, d, (g + 1 if g % 2 else g - 1) % groups, d) for g, d in everywhere])
    face_perms = (twin, along_dev, pair_grp, along_grp)

    def swap(values):
        return [lax.ppermute(v, AXES, perm) for v, perm in zip(values, face_perms)]

    first, *sides = apply_schur(first_kernel, matrix, tests, faces, [], [])
    second, *sides = apply_schur(
        second_kernel, matrix, first, faces, swap(sides), [pltpu.VMEM((rows, columns), BF16)]
    )

    blocks = columns // BLOCK
    unit = 2 * groups * 8
    packed = -(-len(triangle(blocks)) * BLOCK // unit) * unit
    half = packed // 2
    piece = half // groups
    tall, keep, send = call(
        gram_kernel,
        [second, faces, *swap(sides)],
        [((rows, columns), BF16), ((half, BLOCK), F32), ((half, BLOCK), F32)],
        [((packed, BLOCK), F32)],
    )
    got = lax.ppermute(send, AXES, twin)

    def grp_step(step):
        return flat([(g, d, target(g, step, groups), d) for g, d in everywhere])

    def depth_step(step):
        return flat([(g, d, g, 2 * target(d // 2, step, depth) + d % 2) for g, d in everywhere])

    own, *parts = call(
        functools.partial(split_kernel, groups),
        [keep, got],
        [((piece, BLOCK), F32)] + [((piece, BLOCK), BF16)] * (groups - 1),
        [((half, BLOCK), F32)],
    )
    parts = [lax.ppermute(v, AXES, grp_step(i)) for i, v in enumerate(parts, 1)]
    (own,) = call(add_kernel, [own, *parts], [((piece, BLOCK), F32)])
    parts = [lax.ppermute(own, AXES, depth_step(i)) for i in range(1, depth)]
    (own,) = call(
        functools.partial(ordered_kernel, depth),
        [own, *parts],
        [((piece, BLOCK), F32)],
        [((depth * piece, BLOCK), F32)],
    )
    parts = [lax.ppermute(own, AXES, grp_step(i)) for i in range(1, groups)]
    (mine,) = call(functools.partial(join_kernel, groups), [own, *parts], [((half, BLOCK), F32)])
    other = lax.ppermute(mine, AXES, twin)
    basis, factor = call(
        functools.partial(factor_kernel, groups * devs * rows),
        [mine, other, tall],
        [((rows, columns), BF16), ((columns // devs, columns), F32)],
        [((packed, BLOCK), F32), ((columns, columns), F32), ((columns, columns), F32)],
    )
    return basis[None], factor


def solution(mesh):
    return jax.shard_map(
        per_device,
        mesh=mesh,
        in_specs=(P(AXES, None, None),) * 3,
        out_specs=(P(AXES, None, None), P("dev", None)),
        check_vma=False,
    )
```

```python
import functools
import math

import jax
import jax.numpy as jnp
from jax import lax
from jax.experimental import pallas as pl
from jax.experimental.pallas import tpu as pltpu
from jax.sharding import PartitionSpec as P

F32 = jnp.float32
BF16 = jnp.bfloat16
BLOCK = 128
AXES = ("grp", "dev")
VMEM = pl.BlockSpec(memory_space=pltpu.VMEM)
PARAMS = pltpu.CompilerParams(vmem_limit_bytes=20 * 2**20)


def slots_of(face_ref):
    rows = face_ref[...]
    odd_d = lax.rem(lax.axis_index("dev"), 2) == 1
    odd_g = lax.rem(lax.axis_index("grp"), 2) == 1
    f0, f1, f2, f3 = (rows[i : i + 1, :] for i in range(4))
    return (
        jnp.where(odd_d, f0, f1),
        jnp.where(odd_d, f1, f0),
        jnp.where(odd_g, f2, f3),
        jnp.where(odd_g, f3, f2),
    )


def gather_matrix(slots, columns):
    out = []
    for slot in slots:
        count = slot.shape[1]
        column = jnp.transpose(jnp.broadcast_to(slot.astype(F32), (8, count)))[:, 0:1]
        lanes = lax.broadcasted_iota(jnp.int32, (count, columns), 1)
        out.append((column == lanes.astype(F32)).astype(BF16))
    return jnp.concatenate(out, axis=0)


def scatter_matrix(slots, rows):
    out = []
    for slot in slots:
        sub = lax.broadcasted_iota(jnp.int32, (rows, slot.shape[1]), 0)
        out.append((sub == slot).astype(F32).astype(BF16))
    return jnp.concatenate(out, axis=1)


def dot(a, b):
    return jnp.dot(a, b, preferred_element_type=F32)


def contract(a, b, dims, exact=False):
    return lax.dot_general(
        a,
        b,
        (dims, ((), ())),
        precision=lax.Precision.HIGHEST if exact else None,
        preferred_element_type=F32,
    )


def pick(refs):
    return jnp.concatenate([r[...] for r in refs], axis=0)


def spill(value, refs):
    count = refs[0].shape[0]
    for i, ref in enumerate(refs):
        ref[...] = value[i * count : (i + 1) * count].astype(ref.dtype)


def first_kernel(
    schur_hbm, omega_hbm, face_hbm, schur_ref, first_ref, gather, scatter, f0, f1, f2, f3, omega, faces, sems
):
    rows = schur_ref.shape[0]
    steps = sems.shape[0] - 2
    chunk = rows // steps
    face_copy = pltpu.make_async_copy(face_hbm, faces, sems.at[0])
    omega_copy = pltpu.make_async_copy(omega_hbm, omega, sems.at[1])
    face_copy.start()
    omega_copy.start()
    copies = []
    for i in range(steps):
        at = pl.ds(i * chunk, chunk)
        copies.append(pltpu.make_async_copy(schur_hbm.at[at], schur_ref.at[at], sems.at[2 + i]))
        copies[-1].start()
    face_copy.wait()
    slots = slots_of(faces)
    gather[...] = gather_matrix(slots, rows)
    scatter[...] = scatter_matrix(slots, rows)
    omega_copy.wait()
    for i, copy in enumerate(copies):
        copy.wait()
        at = pl.ds(i * chunk, chunk)
        first_ref[at, :] = dot(schur_ref[at, :], omega[...]).astype(BF16)
    spill(dot(gather[...], first_ref[...]), (f0, f1, f2, f3))


def ahead_kernel(schur_ref, first_ref, gather, scatter, whole, side, face_side, face_whole):
    whole[...] = dot(schur_ref[...], first_ref[...])
    side[...] = dot(schur_ref[...], scatter[...]).astype(BF16)
    face_schur = dot(gather[...], schur_ref[...]).astype(BF16)
    face_side[...] = dot(face_schur, scatter[...]).astype(BF16)
    face_whole[...] = dot(face_schur, first_ref[...])


def second_faces_kernel(face_whole, face_side, r0, r1, r2, r3, received, f0, f1, f2, f3):
    received[...] = pick((r0, r1, r2, r3))
    spill(face_whole[...] + dot(face_side[...], received[...]), (f0, f1, f2, f3))


def pack_triangle(packed, value, base=None):
    blocks = value.shape[1] // BLOCK
    side = jnp.transpose(value)
    at = 0
    for i in range(blocks):
        strip = dot(side[i * BLOCK : (i + 1) * BLOCK, :], value[:, i * BLOCK :])
        for j in range(i, blocks):
            part = strip[:, (j - i) * BLOCK : (j - i + 1) * BLOCK]
            here = pl.ds(at * BLOCK, BLOCK)
            packed[here, :] = part if base is None else part + base[here, :]
            at += 1
    spare = packed.shape[0] - at * BLOCK
    if spare:
        packed[pl.ds(at * BLOCK, spare), :] = jnp.zeros((spare, BLOCK), F32)


def inner_kernel(whole, side, received, scatter, inner, packed):
    shared = dot(scatter[...], jnp.ones((scatter.shape[1], BLOCK), BF16))
    shared = jnp.concatenate([shared] * (whole.shape[1] // BLOCK), axis=1)
    second = whole[...] + dot(side[...], received[...])
    inner[...] = jnp.where(shared > 0.5, F32(0.0), second).astype(BF16)
    pack_triangle(packed, inner[...])


def gram_kernel(f0, f1, f2, f3, r0, r1, r2, r3, base, outer, keep_ref, send_ref, packed):
    total = pick((f0, f1, f2, f3)).astype(F32) + pick((r0, r1, r2, r3)).astype(F32)
    outer[...] = (total * F32(1.0 / math.sqrt(2.0))).astype(BF16)
    pack_triangle(packed, outer[...], base)
    half = keep_ref.shape[0]
    core = lax.rem(lax.axis_index("dev"), 2)
    keep_ref[...] = packed[pl.ds(pl.multiple_of(core * half, 8), half), :]
    send_ref[...] = packed[pl.ds(pl.multiple_of((1 - core) * half, 8), half), :].astype(send_ref.dtype)


def tall_kernel(inner, outer, scatter, tall):
    tall[...] = (inner[...].astype(F32) + dot(scatter[...], outer[...])).astype(BF16)


def triangle(count):
    return [(i, j) for i in range(count) for j in range(i, count)]


def partner(index, step, count):
    if count & (count - 1) == 0:
        return index ^ step
    return lax.rem(index + count - step, count) if not isinstance(index, int) else (index - step) % count


def target(index, step, count):
    if count & (count - 1) == 0:
        return index ^ step
    return lax.rem(index + step, count) if not isinstance(index, int) else (index + step) % count


def split_kernel(count, keep_ref, got_ref, own_ref, *rest):
    outs, total = rest[:-1], rest[-1]
    total[...] = keep_ref[...] + got_ref[...].astype(F32)
    me = lax.axis_index("grp")
    size = own_ref.shape[0]
    own_ref[...] = total[pl.ds(pl.multiple_of(me * size, 8), size), :]
    for step, out in enumerate(outs, 1):
        to = target(me, step, count)
        out[...] = total[pl.ds(pl.multiple_of(to * size, 8), size), :].astype(out.dtype)


def add_kernel(*refs):
    total = refs[0][...]
    for ref in refs[1:-1]:
        total = total + ref[...].astype(F32)
    refs[-1][...] = total.astype(refs[-1].dtype)


def ordered_kernel(count, own_ref, *rest):
    got, out_ref, table = rest[:-2], rest[-2], rest[-1]
    me = lax.axis_index("dev") // 2
    size = own_ref.shape[0]

    def put(index, value):
        table[pl.ds(pl.multiple_of(index * size, 8), size), :] = value.astype(F32)

    put(me, own_ref[...])
    for step, ref in enumerate(got, 1):
        put(partner(me, step, count), ref[...])
    total = table[pl.ds(0, size), :]
    for i in range(1, count):
        total = total + table[pl.ds(i * size, size), :]
    out_ref[...] = total.astype(out_ref.dtype)


def join_kernel(count, own_ref, *rest):
    got, out_ref = rest[:-1], rest[-1]
    me = lax.axis_index("grp")
    size = own_ref.shape[0]
    out_ref[pl.ds(pl.multiple_of(me * size, 8), size), :] = own_ref[...]
    for step, ref in enumerate(got, 1):
        out_ref[pl.ds(pl.multiple_of(partner(me, step, count) * size, 8), size), :] = ref[...]


def call(kernel, args, outs, scratch=()):
    return pl.pallas_call(
        kernel,
        in_specs=[VMEM] * len(args),
        out_specs=[VMEM] * len(outs),
        out_shape=[pltpu.VMEM(s, t) for s, t in outs],
        scratch_shapes=[pltpu.VMEM(s, t) for s, t in scratch],
        compiler_params=PARAMS,
    )(*[pltpu.with_memory_space_constraint(x, pltpu.VMEM) for x in args])


def halves(value):
    high = value.astype(BF16)
    return high, (value - high.astype(F32)).astype(BF16)


def dot3(a, b):
    ah, al = halves(a)
    bh, bl = halves(b)
    return dot(jnp.concatenate([ah, ah, al], axis=1), jnp.concatenate([bh, bl, bh], axis=0))


def tdot3(a, b):
    ah, al = halves(a)
    bh, bl = halves(b)
    return contract(
        jnp.concatenate([ah, ah, al], axis=0), jnp.concatenate([bh, bl, bh], axis=0), ((0,), (0,))
    )


PANEL = 8
STRIPE = 64


def eliminate(block, put):
    size = block.shape[0]
    lane = lax.broadcasted_iota(jnp.int32, (1, size), 1)
    cell = lax.broadcasted_iota(jnp.int32, (PANEL, size), 1) - lax.broadcasted_iota(
        jnp.int32, (PANEL, size), 0
    )
    near = min(STRIPE + PANEL, size)
    rows, far = block[:near], block[near:]
    ahead, left, right = None, [], []
    for c in range(0, size, PANEL):
        end = (c // STRIPE + 1) * STRIPE
        wide = [jnp.broadcast_to(rows[:, c + j : c + j + 1], rows.shape) for j in range(PANEL)]
        top = [x[:PANEL] for x in wide] if ahead is None else ahead
        rest = [x[PANEL:] for x in wide]
        last = c + PANEL == size
        here = (lane >= c) & (lane < c + PANEL)
        panel = jnp.where(here, (cell == c).astype(F32), rows[:PANEL])
        if not last:
            below = rows[PANEL:]
            ahead = [
                jnp.broadcast_to(below[:PANEL, at : at + 1], (PANEL, size))
                for at in range(c + PANEL, c + 2 * PANEL)
            ]
            below = jnp.where(here, F32(0.0), below)
        done = []
        for j in range(PANEL):
            scale = lax.rsqrt(top[j][j : j + 1, :])
            row = panel[j : j + 1, :] * scale
            put(c + j, row)
            done.append(row)
            lower = top[j] * scale
            panel = panel - lower * row
            ups = {i: top[i][j : j + 1, :] * scale for i in range(j + 1, PANEL)}
            for i, up in ups.items():
                top[i] = top[i] - lower * up
            if not last:
                lower = rest[j] * scale
                below = below - lower * row
                for i, up in ups.items():
                    rest[i] = rest[i] - lower * up
                lower = lower[:PANEL]
                ahead = [x - lower * lower[i : i + 1, :] for i, x in enumerate(ahead)]
        if last:
            break
        rows = below
        if far.shape[0]:
            done = jnp.concatenate(done, axis=0)
            left.append(done)
            right.append(jnp.where((lane >= c + PANEL) & (lane < end), F32(0.0), done))
            if c + PANEL == end:
                change = tdot3(jnp.concatenate(left, axis=0), jnp.concatenate(right, axis=0))[near:]
                far = jnp.where((lane >= end - STRIPE) & (lane < end), F32(0.0), far) - change
                more = min(end + STRIPE + PANEL, size) - near
                rows = jnp.concatenate([rows, far[:more]], axis=0)
                far, near, left, right = far[more:], near + more, [], []


def factor_kernel(
    total_rows, own_ref, other_ref, tall_ref, basis_hbm, factor_hbm, packed, upper, inverse, basis, sems
):
    half = own_ref.shape[0]
    core = lax.rem(lax.axis_index("dev"), 2)
    packed[pl.ds(pl.multiple_of(core * half, 8), half), :] = own_ref[...].astype(F32)
    packed[pl.ds(pl.multiple_of((1 - core) * half, 8), half), :] = other_ref[...].astype(F32)
    columns = tall_ref.shape[1]
    blocks = columns // BLOCK
    span = lambda i: pl.ds(i * BLOCK, BLOCK)
    gram = {
        pair: packed[span(at), :] * F32(1.0 / total_rows) for at, pair in enumerate(triangle(blocks))
    }
    row = lax.broadcasted_iota(jnp.int32, (BLOCK, BLOCK), 0)
    column = lax.broadcasted_iota(jnp.int32, (BLOCK, BLOCK), 1)
    upper[...] = jnp.zeros(upper.shape, F32)
    copies = []
    for b in range(blocks):
        here = slice(b * BLOCK, (b + 1) * BLOCK)

        def put(i, value):
            inverse[pl.ds(b * BLOCK + i, 1), here] = value

        eliminate(gram[b, b], put)
        diagonal = jnp.where(row >= column, inverse[here, here], F32(0.0))
        strip = {j: dot3(diagonal, gram[b, j]) for j in range(b + 1, blocks)}
        for i in range(b + 1, blocks):
            for j in range(i, blocks):
                gram[i, j] = gram[i, j] - tdot3(strip[i], strip[j])
        for j, value in strip.items():
            upper[here, j * BLOCK : (j + 1) * BLOCK] = value
        corner = contract(diagonal, gram[b, b], ((1,), (0,)), exact=True)
        upper[here, here] = jnp.where(row <= column, corner, F32(0.0))
        inverse[here, here] = diagonal
        if b:
            before = slice(0, b * BLOCK)
            mixed = tdot3(upper[before, here], inverse[before, before])
            inverse[here, before] = -dot3(diagonal, mixed)
        reach = slice(0, (b + 1) * BLOCK)
        basis[:, here] = contract(
            tall_ref[:, reach], inverse[here, reach].astype(BF16), ((1,), (1,))
        ).astype(BF16)
        copies.append(pltpu.make_async_copy(basis.at[:, here], basis_hbm.at[:, here], sems.at[b]))
        copies[-1].start()
        if b + 1 < blocks:
            inverse[here, (b + 1) * BLOCK :] = jnp.zeros((BLOCK, columns - (b + 1) * BLOCK), F32)
    share = factor_hbm.shape[0]
    mine = pl.ds(pl.multiple_of(lax.axis_index("dev") * share, 8), share)
    copies.append(pltpu.make_async_copy(upper.at[mine], factor_hbm, sems.at[blocks]))
    copies[-1].start()
    for copy in copies:
        copy.wait()


def per_device(schur, omega, face_rows):
    matrix, tests, faces = schur[0], omega[0], face_rows[0]
    groups = lax.axis_size("grp")
    devs = lax.axis_size("dev")
    depth = devs // 2
    rows, columns = tests.shape
    inner_size = matrix.shape[1]
    count = faces.shape[1]
    shared = 4 * count

    def flat(pairs):
        return [(g * devs + d, h * devs + e) for g, d, h, e in pairs]

    everywhere = [(g, d) for g in range(groups) for d in range(devs)]
    twin = flat([(g, d, g, d ^ 1) for g, d in everywhere])
    along_dev = flat([(g, d, g, (d + 1 if d % 2 else d - 1) % devs) for g, d in everywhere])
    pair_grp = flat([(g, d, g ^ 1, d) for g, d in everywhere])
    along_grp = flat([(g, d, (g + 1 if g % 2 else g - 1) % groups, d) for g, d in everywhere])
    face_perms = (twin, along_dev, pair_grp, along_grp)

    def swap(values):
        return [lax.ppermute(v, AXES, perm) for v, perm in zip(values, face_perms)]

    face_outs = [((count, columns), BF16)] * 4
    steps = 4 if rows % (4 * 16) == 0 else 1
    schur_v, first, gather, scatter, *sides = pl.pallas_call(
        first_kernel,
        in_specs=[pl.BlockSpec(memory_space=pltpu.HBM)] * 3,
        out_specs=[VMEM] * 8,
        out_shape=[
            pltpu.VMEM(s, t)
            for s, t in [
                ((rows, inner_size), BF16),
                ((rows, columns), BF16),
                ((shared, rows), BF16),
                ((rows, shared), BF16),
                *face_outs,
            ]
        ],
        scratch_shapes=[
            pltpu.VMEM((rows, columns), BF16),
            pltpu.VMEM(faces.shape, jnp.int32),
            pltpu.SemaphoreType.DMA((2 + steps,)),
        ],
        compiler_params=PARAMS,
    )(*[pltpu.with_memory_space_constraint(x, pltpu.HBM) for x in (matrix, tests, faces)])
    got = swap(sides)
    whole, side, face_side, face_whole = call(
        ahead_kernel,
        [schur_v, first, gather, scatter],
        [
            ((rows, columns), F32),
            ((rows, shared), BF16),
            ((shared, shared), BF16),
            ((shared, columns), F32),
        ],
    )
    received, *sides = call(
        second_faces_kernel, [face_whole, face_side, *got], [((shared, columns), BF16), *face_outs]
    )
    got = swap(sides)

    blocks = columns // BLOCK
    unit = 2 * groups * 8
    packed = -(-len(triangle(blocks)) * BLOCK // unit) * unit
    half = packed // 2
    piece = half // groups
    inner, base = call(
        inner_kernel,
        [whole, side, received, scatter],
        [((rows, columns), BF16), ((packed, BLOCK), F32)],
    )
    outer, keep, send = call(
        gram_kernel,
        [*sides, *got, base],
        [((shared, columns), BF16), ((half, BLOCK), F32), ((half, BLOCK), F32)],
        [((packed, BLOCK), F32)],
    )
    got = lax.ppermute(send, AXES, twin)
    (tall,) = call(tall_kernel, [inner, outer, scatter], [((rows, columns), BF16)])

    def grp_step(step):
        return flat([(g, d, target(g, step, groups), d) for g, d in everywhere])

    def depth_step(step):
        return flat([(g, d, g, 2 * target(d // 2, step, depth) + d % 2) for g, d in everywhere])

    own, *parts = call(
        functools.partial(split_kernel, groups),
        [keep, got],
        [((piece, BLOCK), F32)] + [((piece, BLOCK), BF16)] * (groups - 1),
        [((half, BLOCK), F32)],
    )
    parts = [lax.ppermute(v, AXES, grp_step(i)) for i, v in enumerate(parts, 1)]
    (own,) = call(add_kernel, [own, *parts], [((piece, BLOCK), BF16)])
    parts = [lax.ppermute(own, AXES, depth_step(i)) for i in range(1, depth)]
    (own,) = call(
        functools.partial(ordered_kernel, depth),
        [own, *parts],
        [((piece, BLOCK), F32)],
        [((depth * piece, BLOCK), F32)],
    )
    parts = [lax.ppermute(own, AXES, grp_step(i)) for i in range(1, groups)]
    (mine,) = call(functools.partial(join_kernel, groups), [own, *parts], [((half, BLOCK), F32)])
    other = lax.ppermute(mine, AXES, twin)
    basis, factor = pl.pallas_call(
        functools.partial(factor_kernel, groups * devs * rows),
        in_specs=[VMEM] * 3,
        out_specs=[pl.BlockSpec(memory_space=pl.ANY)] * 2,
        out_shape=[
            jax.ShapeDtypeStruct((rows, columns), BF16),
            jax.ShapeDtypeStruct((columns // devs, columns), F32),
        ],
        scratch_shapes=[
            pltpu.VMEM((packed, BLOCK), F32),
            pltpu.VMEM((columns, columns), F32),
            pltpu.VMEM((columns, columns), F32),
            pltpu.VMEM((rows, columns), BF16),
            pltpu.SemaphoreType.DMA((blocks + 1,)),
        ],
        compiler_params=PARAMS,
    )(*[pltpu.with_memory_space_constraint(x, pltpu.VMEM) for x in (mine, other, tall)])
    return basis[None], factor


def solution(mesh):
    return jax.shard_map(
        per_device,
        mesh=mesh,
        in_specs=(P(AXES, None, None),) * 3,
        out_specs=(P(AXES, None, None), P("dev", None)),
        check_vma=False,
    )
```

```python
import functools
import math

import jax
import jax.numpy as jnp
from jax import lax
from jax.experimental import pallas as pl
from jax.experimental.pallas import tpu as pltpu
from jax.sharding import PartitionSpec as P

F32 = jnp.float32
BF16 = jnp.bfloat16
BLOCK = 128
AXES = ("grp", "dev")
VMEM = pl.BlockSpec(memory_space=pltpu.VMEM)
PARAMS = pltpu.CompilerParams(vmem_limit_bytes=20 * 2**20)


def slots_of(face_ref):
    rows = face_ref[...]
    odd_d = lax.rem(lax.axis_index("dev"), 2) == 1
    odd_g = lax.rem(lax.axis_index("grp"), 2) == 1
    f0, f1, f2, f3 = (rows[i : i + 1, :] for i in range(4))
    return (
        jnp.where(odd_g, f3, f2),
        jnp.where(odd_g, f2, f3),
        jnp.where(odd_d, f1, f0),
        jnp.where(odd_d, f0, f1),
    )


def gather_matrix(slots, columns):
    out = []
    for slot in slots:
        count = slot.shape[1]
        column = jnp.transpose(jnp.broadcast_to(slot.astype(F32), (8, count)))[:, 0:1]
        lanes = lax.broadcasted_iota(jnp.int32, (count, columns), 1)
        out.append((column == lanes.astype(F32)).astype(BF16))
    return jnp.concatenate(out, axis=0)


def scatter_matrix(slots, rows):
    out = []
    for slot in slots:
        sub = lax.broadcasted_iota(jnp.int32, (rows, slot.shape[1]), 0)
        out.append((sub == slot).astype(F32).astype(BF16))
    return jnp.concatenate(out, axis=1)


def dot(a, b):
    return jnp.dot(a, b, preferred_element_type=F32)


def contract(a, b, dims, exact=False):
    return lax.dot_general(
        a,
        b,
        (dims, ((), ())),
        precision=lax.Precision.HIGHEST if exact else None,
        preferred_element_type=F32,
    )


def pick(refs):
    return jnp.concatenate([r[...] for r in refs], axis=0)


def spill(value, refs):
    count = refs[0].shape[0]
    for i, ref in enumerate(refs):
        ref[...] = value[i * count : (i + 1) * count].astype(ref.dtype)


def first_kernel(
    schur_hbm, omega_hbm, face_hbm, schur_ref, first_ref, gather, faces, f0, f1, f2, f3, omega, sems
):
    rows = schur_ref.shape[0]
    steps = sems.shape[0] - 2
    chunk = rows // steps
    face_copy = pltpu.make_async_copy(face_hbm, faces, sems.at[0])
    omega_copy = pltpu.make_async_copy(omega_hbm, omega, sems.at[1])
    face_copy.start()
    omega_copy.start()
    copies = []
    for i in range(steps):
        at = pl.ds(i * chunk, chunk)
        copies.append(pltpu.make_async_copy(schur_hbm.at[at], schur_ref.at[at], sems.at[2 + i]))
        copies[-1].start()
    face_copy.wait()
    gather[...] = gather_matrix(slots_of(faces), rows)
    omega_copy.wait()
    for i, copy in enumerate(copies):
        copy.wait()
        at = pl.ds(i * chunk, chunk)
        first_ref[at, :] = dot(schur_ref[at, :], omega[...]).astype(BF16)
    spill(dot(gather[...], first_ref[...]), (f0, f1, f2, f3))


def ahead_kernel(schur_ref, first_ref, gather, faces, scatter, whole, face_side, face_whole):
    scatter[...] = scatter_matrix(slots_of(faces), schur_ref.shape[0])
    face_schur = dot(gather[...], schur_ref[...]).astype(BF16)
    face_whole[...] = dot(face_schur, first_ref[...])
    face_side[...] = dot(face_schur, scatter[...]).astype(BF16)
    whole[...] = dot(schur_ref[...], first_ref[...])


def second_faces_kernel(face_whole, face_side, r0, r1, r2, r3, received, f0, f1, f2, f3):
    received[...] = pick((r0, r1, r2, r3))
    spill(face_whole[...] + dot(face_side[...], received[...]), (f0, f1, f2, f3))


def pack_triangle(packed, value, base=None):
    blocks = value.shape[1] // BLOCK
    side = jnp.transpose(value)
    at = 0
    for i in range(blocks):
        strip = dot(side[i * BLOCK : (i + 1) * BLOCK, :], value[:, i * BLOCK :])
        for j in range(i, blocks):
            part = strip[:, (j - i) * BLOCK : (j - i + 1) * BLOCK]
            here = pl.ds(at * BLOCK, BLOCK)
            packed[here, :] = part if base is None else part + base[here, :]
            at += 1
    spare = packed.shape[0] - at * BLOCK
    if spare:
        packed[pl.ds(at * BLOCK, spare), :] = jnp.zeros((spare, BLOCK), F32)


def inner_kernel(schur_ref, whole, received, scatter, inner, packed):
    shared = dot(scatter[...], jnp.ones((scatter.shape[1], BLOCK), BF16))
    shared = jnp.concatenate([shared] * (whole.shape[1] // BLOCK), axis=1)
    side = dot(schur_ref[...], scatter[...]).astype(BF16)
    second = whole[...] + dot(side, received[...])
    inner[...] = jnp.where(shared > 0.5, F32(0.0), second).astype(BF16)
    pack_triangle(packed, inner[...])


def gram_kernel(f0, f1, f2, f3, r0, r1, r2, r3, base, outer, keep_ref, send_ref, packed):
    total = pick((f0, f1, f2, f3)).astype(F32) + pick((r0, r1, r2, r3)).astype(F32)
    outer[...] = (total * F32(1.0 / math.sqrt(2.0))).astype(BF16)
    pack_triangle(packed, outer[...], base)
    half = keep_ref.shape[0]
    core = lax.rem(lax.axis_index("dev"), 2)
    keep_ref[...] = packed[pl.ds(pl.multiple_of(core * half, 8), half), :]
    send_ref[...] = packed[pl.ds(pl.multiple_of((1 - core) * half, 8), half), :].astype(send_ref.dtype)


def tall_kernel(inner, outer, scatter, tall):
    tall[...] = (inner[...].astype(F32) + dot(scatter[...], outer[...])).astype(BF16)


def triangle(count):
    return [(i, j) for i in range(count) for j in range(i, count)]


def partner(index, step, count):
    if count & (count - 1) == 0:
        return index ^ step
    return lax.rem(index + count - step, count) if not isinstance(index, int) else (index - step) % count


def target(index, step, count):
    if count & (count - 1) == 0:
        return index ^ step
    return lax.rem(index + step, count) if not isinstance(index, int) else (index + step) % count


def split_kernel(count, keep_ref, got_ref, own_ref, *rest):
    outs, total = rest[:-1], rest[-1]
    total[...] = keep_ref[...] + got_ref[...].astype(F32)
    me = lax.axis_index("grp")
    size = own_ref.shape[0]
    own_ref[...] = total[pl.ds(pl.multiple_of(me * size, 8), size), :]
    for step, out in enumerate(outs, 1):
        to = target(me, step, count)
        out[...] = total[pl.ds(pl.multiple_of(to * size, 8), size), :].astype(out.dtype)


def add_kernel(*refs):
    total = refs[0][...]
    for ref in refs[1:-1]:
        total = total + ref[...].astype(F32)
    refs[-1][...] = total.astype(refs[-1].dtype)


def ordered_kernel(count, own_ref, *rest):
    got, out_ref, table = rest[:-2], rest[-2], rest[-1]
    me = lax.axis_index("dev") // 2
    size = own_ref.shape[0]

    def put(index, value):
        table[pl.ds(pl.multiple_of(index * size, 8), size), :] = value.astype(F32)

    put(me, own_ref[...])
    for step, ref in enumerate(got, 1):
        put(partner(me, step, count), ref[...])
    total = table[pl.ds(0, size), :]
    for i in range(1, count):
        total = total + table[pl.ds(i * size, size), :]
    out_ref[...] = total.astype(out_ref.dtype)


def call(kernel, args, outs, scratch=()):
    return pl.pallas_call(
        kernel,
        in_specs=[VMEM] * len(args),
        out_specs=[VMEM] * len(outs),
        out_shape=[pltpu.VMEM(s, t) for s, t in outs],
        scratch_shapes=[pltpu.VMEM(s, t) for s, t in scratch],
        compiler_params=PARAMS,
    )(*[pltpu.with_memory_space_constraint(x, pltpu.VMEM) for x in args])


def halves(value):
    high = value.astype(BF16)
    return high, (value - high.astype(F32)).astype(BF16)


def dot3(a, b):
    ah, al = halves(a)
    bh, bl = halves(b)
    return dot(jnp.concatenate([ah, ah, al], axis=1), jnp.concatenate([bh, bl, bh], axis=0))


def tdot3(a, b):
    ah, al = halves(a)
    bh, bl = halves(b)
    return contract(
        jnp.concatenate([ah, ah, al], axis=0), jnp.concatenate([bh, bl, bh], axis=0), ((0,), (0,))
    )


PANEL = 8
STRIPE = 64


def eliminate(block, put):
    size = block.shape[0]
    lane = lax.broadcasted_iota(jnp.int32, (1, size), 1)
    cell = lax.broadcasted_iota(jnp.int32, (PANEL, size), 1) - lax.broadcasted_iota(
        jnp.int32, (PANEL, size), 0
    )
    near = min(STRIPE + PANEL, size)
    rows, far = block[:near], block[near:]
    ahead, left, right = None, [], []
    for c in range(0, size, PANEL):
        end = (c // STRIPE + 1) * STRIPE
        wide = [jnp.broadcast_to(rows[:, c + j : c + j + 1], rows.shape) for j in range(PANEL)]
        top = [x[:PANEL] for x in wide] if ahead is None else ahead
        rest = [x[PANEL:] for x in wide]
        last = c + PANEL == size
        here = (lane >= c) & (lane < c + PANEL)
        panel = jnp.where(here, (cell == c).astype(F32), rows[:PANEL])
        if not last:
            below = rows[PANEL:]
            ahead = [
                jnp.broadcast_to(below[:PANEL, at : at + 1], (PANEL, size))
                for at in range(c + PANEL, c + 2 * PANEL)
            ]
            below = jnp.where(here, F32(0.0), below)
        done = []
        for j in range(PANEL):
            scale = lax.rsqrt(top[j][j : j + 1, :])
            row = panel[j : j + 1, :] * scale
            put(c + j, row)
            done.append(row)
            lower = top[j] * scale
            panel = panel - lower * row
            ups = {i: top[i][j : j + 1, :] * scale for i in range(j + 1, PANEL)}
            for i, up in ups.items():
                top[i] = top[i] - lower * up
            if not last:
                lower = rest[j] * scale
                below = below - lower * row
                for i, up in ups.items():
                    rest[i] = rest[i] - lower * up
                lower = lower[:PANEL]
                ahead = [x - lower * lower[i : i + 1, :] for i, x in enumerate(ahead)]
        if last:
            break
        rows = below
        if far.shape[0]:
            done = jnp.concatenate(done, axis=0)
            left.append(done)
            right.append(jnp.where((lane >= c + PANEL) & (lane < end), F32(0.0), done))
            if c + PANEL == end:
                change = tdot3(jnp.concatenate(left, axis=0), jnp.concatenate(right, axis=0))[near:]
                far = jnp.where((lane >= end - STRIPE) & (lane < end), F32(0.0), far) - change
                more = min(end + STRIPE + PANEL, size) - near
                rows = jnp.concatenate([rows, far[:more]], axis=0)
                far, near, left, right = far[more:], near + more, [], []


def factor_kernel(total_rows, groups, tall_ref, *rest):
    mine, other = rest[:groups], rest[groups : 2 * groups]
    basis_hbm, factor_hbm, packed, upper, inverse, basis, sems = rest[2 * groups :]
    me = lax.axis_index("grp")
    core = lax.rem(lax.axis_index("dev"), 2)
    size = mine[0].shape[0]
    for at, refs in ((core, mine), (1 - core, other)):
        for step, ref in enumerate(refs):
            place = at * groups + (partner(me, step, groups) if step else me)
            packed[pl.ds(pl.multiple_of(place * size, 8), size), :] = ref[...]
    columns = tall_ref.shape[1]
    blocks = columns // BLOCK
    span = lambda i: pl.ds(i * BLOCK, BLOCK)
    gram = {
        pair: packed[span(at), :] * F32(1.0 / total_rows) for at, pair in enumerate(triangle(blocks))
    }
    row = lax.broadcasted_iota(jnp.int32, (BLOCK, BLOCK), 0)
    column = lax.broadcasted_iota(jnp.int32, (BLOCK, BLOCK), 1)
    copies = []
    for b in range(blocks):
        here = slice(b * BLOCK, (b + 1) * BLOCK)
        before = slice(0, b * BLOCK)
        last = b + 1 == blocks

        def put(i, value):
            inverse[pl.ds(b * BLOCK + i, 1), here] = value

        mixed = tdot3(upper[before, here], inverse[before, before]) if b else None
        if last and b:
            kept = contract(tall_ref[:, before], mixed.astype(BF16), ((1,), (1,)))
            rest = jnp.concatenate(halves(tall_ref[:, here].astype(F32) - kept), axis=1)
        eliminate(gram[b, b], put)
        diagonal = jnp.where(row >= column, inverse[here, here], F32(0.0))
        strip = {j: dot3(diagonal, gram[b, j]) for j in range(b + 1, blocks)}
        for i in range(b + 1, blocks):
            for j in range(i, blocks):
                gram[i, j] = gram[i, j] - tdot3(strip[i], strip[j])
        for j, value in strip.items():
            upper[here, j * BLOCK : (j + 1) * BLOCK] = value
        if last and b:
            narrow = diagonal.astype(BF16)
            value = contract(rest, jnp.concatenate([narrow, narrow], axis=1), ((1,), (1,)))
        else:
            reach = slice(0, (b + 1) * BLOCK)
            inverse[here, here] = diagonal
            if b:
                inverse[here, before] = -dot3(diagonal, mixed)
            if not last:
                inverse[here, (b + 1) * BLOCK :] = jnp.zeros((BLOCK, columns - (b + 1) * BLOCK), F32)
            value = contract(tall_ref[:, reach], inverse[here, reach].astype(BF16), ((1,), (1,)))
        basis[:, here] = value.astype(BF16)
        copies.append(pltpu.make_async_copy(basis.at[:, here], basis_hbm.at[:, here], sems.at[b]))
        copies[-1].start()
        corner = dot3(diagonal, gram[b, b])
        upper[here, here] = jnp.where(row <= column, corner, F32(0.0))
        if b:
            upper[here, before] = jnp.zeros((BLOCK, b * BLOCK), F32)
    share = factor_hbm.shape[0]
    mine = pl.ds(pl.multiple_of(lax.axis_index("dev") * share, 8), share)
    copies.append(pltpu.make_async_copy(upper.at[mine], factor_hbm, sems.at[blocks]))
    copies[-1].start()
    for copy in copies:
        copy.wait()


def per_device(schur, omega, face_rows):
    matrix, tests, faces = schur[0], omega[0], face_rows[0]
    groups = lax.axis_size("grp")
    devs = lax.axis_size("dev")
    depth = devs // 2
    rows, columns = tests.shape
    inner_size = matrix.shape[1]
    count = faces.shape[1]
    shared = 4 * count

    def flat(pairs):
        return [(g * devs + d, h * devs + e) for g, d, h, e in pairs]

    everywhere = [(g, d) for g in range(groups) for d in range(devs)]
    twin = flat([(g, d, g, d ^ 1) for g, d in everywhere])
    along_dev = flat([(g, d, g, (d + 1 if d % 2 else d - 1) % devs) for g, d in everywhere])
    pair_grp = flat([(g, d, g ^ 1, d) for g, d in everywhere])
    along_grp = flat([(g, d, (g + 1 if g % 2 else g - 1) % groups, d) for g, d in everywhere])
    face_perms = (along_grp, pair_grp, along_dev, twin)

    def swap(values):
        return [lax.ppermute(v, AXES, perm) for v, perm in zip(values, face_perms)]

    face_outs = [((count, columns), BF16)] * 4
    steps = 2 if rows % 256 == 0 else 1
    schur_v, first, gather, faces_v, *sides = pl.pallas_call(
        first_kernel,
        in_specs=[pl.BlockSpec(memory_space=pltpu.HBM)] * 3,
        out_specs=[VMEM] * (4 + len(face_outs)),
        out_shape=[
            pltpu.VMEM(s, t)
            for s, t in [
                ((rows, inner_size), BF16),
                ((rows, columns), BF16),
                ((shared, rows), BF16),
                (faces.shape, jnp.int32),
                *face_outs,
            ]
        ],
        scratch_shapes=[
            pltpu.VMEM((rows, columns), BF16),
            pltpu.SemaphoreType.DMA((2 + steps,)),
        ],
        compiler_params=PARAMS,
    )(*[pltpu.with_memory_space_constraint(x, pltpu.HBM) for x in (matrix, tests, faces)])
    got = swap(sides)
    scatter, whole, face_side, face_whole = call(
        ahead_kernel,
        [schur_v, first, gather, faces_v],
        [
            ((rows, shared), BF16),
            ((rows, columns), F32),
            ((shared, shared), BF16),
            ((shared, columns), F32),
        ],
    )
    received, *sides = call(
        second_faces_kernel, [face_whole, face_side, *got], [((shared, columns), BF16), *face_outs]
    )
    got = swap(sides)

    blocks = columns // BLOCK
    unit = 2 * groups * 8
    packed = -(-len(triangle(blocks)) * BLOCK // unit) * unit
    half = packed // 2
    piece = half // groups
    inner, base = call(
        inner_kernel,
        [schur_v, whole, received, scatter],
        [((rows, columns), BF16), ((packed, BLOCK), F32)],
    )
    outer, keep, send = call(
        gram_kernel,
        [*sides, *got, base],
        [((shared, columns), BF16), ((half, BLOCK), F32), ((half, BLOCK), F32)],
        [((packed, BLOCK), F32)],
    )
    got = lax.ppermute(send, AXES, twin)
    (tall,) = call(tall_kernel, [inner, outer, scatter], [((rows, columns), BF16)])

    def grp_step(step):
        return flat([(g, d, target(g, step, groups), d) for g, d in everywhere])

    def depth_step(step):
        return flat([(g, d, g, 2 * target(d // 2, step, depth) + d % 2) for g, d in everywhere])

    own, *parts = call(
        functools.partial(split_kernel, groups),
        [keep, got],
        [((piece, BLOCK), F32)] + [((piece, BLOCK), BF16)] * (groups - 1),
        [((half, BLOCK), F32)],
    )
    parts = [lax.ppermute(v, AXES, grp_step(i)) for i, v in enumerate(parts, 1)]
    (own,) = call(add_kernel, [own, *parts], [((piece, BLOCK), BF16)])
    parts = [lax.ppermute(own, AXES, depth_step(i)) for i in range(1, depth)]
    (own,) = call(
        functools.partial(ordered_kernel, depth),
        [own, *parts],
        [((piece, BLOCK), F32)],
        [((depth * piece, BLOCK), F32)],
    )
    parts = [lax.ppermute(own, AXES, grp_step(i)) for i in range(1, groups)]
    mine = [own, *parts]
    other = [lax.ppermute(v, AXES, twin) for v in mine]
    basis, factor = pl.pallas_call(
        functools.partial(factor_kernel, groups * devs * rows, groups),
        in_specs=[VMEM] * (1 + 2 * groups),
        out_specs=[pl.BlockSpec(memory_space=pl.ANY)] * 2,
        out_shape=[
            jax.ShapeDtypeStruct((rows, columns), BF16),
            jax.ShapeDtypeStruct((columns // devs, columns), F32),
        ],
        scratch_shapes=[
            pltpu.VMEM((packed, BLOCK), F32),
            pltpu.VMEM((columns, columns), F32),
            pltpu.VMEM((columns, columns), F32),
            pltpu.VMEM((rows, columns), BF16),
            pltpu.SemaphoreType.DMA((blocks + 1,)),
        ],
        compiler_params=PARAMS,
    )(*[pltpu.with_memory_space_constraint(x, pltpu.VMEM) for x in (tall, *mine, *other)])
    return basis[None], factor


def solution(mesh):
    return jax.shard_map(
        per_device,
        mesh=mesh,
        in_specs=(P(AXES, None, None),) * 3,
        out_specs=(P(AXES, None, None), P("dev", None)),
        check_vma=False,
    )
```

```python
import functools
import math

import jax
import jax.numpy as jnp
from jax import lax
from jax.experimental import pallas as pl
from jax.experimental.pallas import tpu as pltpu
from jax.sharding import PartitionSpec as P

F32 = jnp.float32
BF16 = jnp.bfloat16
BLOCK = 128
AXES = ("grp", "dev")
VMEM = pl.BlockSpec(memory_space=pltpu.VMEM)
PARAMS = pltpu.CompilerParams(vmem_limit_bytes=20 * 2**20)


def slots_of(face_ref):
    rows = face_ref[...]
    odd_d = lax.rem(lax.axis_index("dev"), 2) == 1
    odd_g = lax.rem(lax.axis_index("grp"), 2) == 1
    f0, f1, f2, f3 = (rows[i : i + 1, :] for i in range(4))
    return (
        jnp.where(odd_g, f3, f2),
        jnp.where(odd_g, f2, f3),
        jnp.where(odd_d, f1, f0),
        jnp.where(odd_d, f0, f1),
    )


def gather_matrix(slots, columns):
    out = []
    for slot in slots:
        count = slot.shape[1]
        column = jnp.transpose(jnp.broadcast_to(slot.astype(F32), (8, count)))[:, 0:1]
        lanes = lax.broadcasted_iota(jnp.int32, (count, columns), 1)
        out.append((column == lanes.astype(F32)).astype(BF16))
    return jnp.concatenate(out, axis=0)


def scatter_matrix(slots, rows):
    out = []
    for slot in slots:
        sub = lax.broadcasted_iota(jnp.int32, (rows, slot.shape[1]), 0)
        out.append((sub == slot).astype(F32).astype(BF16))
    return jnp.concatenate(out, axis=1)


def dot(a, b):
    return jnp.dot(a, b, preferred_element_type=F32)


def contract(a, b, dims, exact=False):
    return lax.dot_general(
        a,
        b,
        (dims, ((), ())),
        precision=lax.Precision.HIGHEST if exact else None,
        preferred_element_type=F32,
    )


def pick(refs):
    return jnp.concatenate([r[...] for r in refs], axis=0)


def spill(value, refs):
    count = refs[0].shape[0]
    for i, ref in enumerate(refs):
        ref[...] = value[i * count : (i + 1) * count].astype(ref.dtype)


def first_kernel(
    schur_hbm, omega_hbm, face_hbm, schur_ref, first_ref, gather, faces, f0, f1, f2, f3, omega, sems
):
    rows = schur_ref.shape[0]
    steps = sems.shape[0] - 2
    chunk = rows // steps
    face_copy = pltpu.make_async_copy(face_hbm, faces, sems.at[0])
    omega_copy = pltpu.make_async_copy(omega_hbm, omega, sems.at[1])
    face_copy.start()
    omega_copy.start()
    copies = []
    for i in range(steps):
        at = pl.ds(i * chunk, chunk)
        copies.append(pltpu.make_async_copy(schur_hbm.at[at], schur_ref.at[at], sems.at[2 + i]))
        copies[-1].start()
    face_copy.wait()
    gather[...] = gather_matrix(slots_of(faces), rows)
    omega_copy.wait()
    for i, copy in enumerate(copies):
        copy.wait()
        at = pl.ds(i * chunk, chunk)
        first_ref[at, :] = dot(schur_ref[at, :], omega[...]).astype(BF16)
    spill(dot(gather[...], first_ref[...]), (f0, f1, f2, f3))


def ahead_kernel(schur_ref, first_ref, gather, faces, scatter, whole, face_side, face_whole):
    scatter[...] = scatter_matrix(slots_of(faces), schur_ref.shape[0])
    face_schur = dot(gather[...], schur_ref[...]).astype(BF16)
    face_whole[...] = dot(face_schur, first_ref[...])
    face_side[...] = dot(face_schur, scatter[...]).astype(BF16)
    whole[...] = dot(schur_ref[...], first_ref[...])


def second_faces_kernel(face_whole, face_side, r0, r1, r2, r3, received, f0, f1, f2, f3):
    received[...] = pick((r0, r1, r2, r3))
    spill(face_whole[...] + dot(face_side[...], received[...]), (f0, f1, f2, f3))


def pack_triangle(packed, value, base=None):
    blocks = value.shape[1] // BLOCK
    side = jnp.transpose(value)
    at = 0
    for i in range(blocks):
        strip = dot(side[i * BLOCK : (i + 1) * BLOCK, :], value[:, i * BLOCK :])
        for j in range(i, blocks):
            part = strip[:, (j - i) * BLOCK : (j - i + 1) * BLOCK]
            here = pl.ds(at * BLOCK, BLOCK)
            packed[here, :] = part if base is None else part + base[here, :]
            at += 1
    spare = packed.shape[0] - at * BLOCK
    if spare:
        packed[pl.ds(at * BLOCK, spare), :] = jnp.zeros((spare, BLOCK), F32)


def inner_kernel(schur_ref, whole, received, scatter, inner, packed):
    shared = dot(scatter[...], jnp.ones((scatter.shape[1], BLOCK), BF16))
    shared = jnp.concatenate([shared] * (whole.shape[1] // BLOCK), axis=1)
    side = dot(schur_ref[...], scatter[...]).astype(BF16)
    second = whole[...] + dot(side, received[...])
    inner[...] = jnp.where(shared > 0.5, F32(0.0), second).astype(BF16)
    pack_triangle(packed, inner[...])


def gram_kernel(f0, f1, f2, f3, r0, r1, r2, r3, base, outer, keep_ref, send_ref, packed):
    total = pick((f0, f1, f2, f3)).astype(F32) + pick((r0, r1, r2, r3)).astype(F32)
    outer[...] = (total * F32(1.0 / math.sqrt(2.0))).astype(BF16)
    pack_triangle(packed, outer[...], base)
    half = keep_ref.shape[0]
    core = lax.rem(lax.axis_index("dev"), 2)
    keep_ref[...] = packed[pl.ds(pl.multiple_of(core * half, 8), half), :]
    send_ref[...] = packed[pl.ds(pl.multiple_of((1 - core) * half, 8), half), :].astype(send_ref.dtype)


def tall_kernel(inner, outer, scatter, tall):
    tall[...] = (inner[...].astype(F32) + dot(scatter[...], outer[...])).astype(BF16)


def triangle(count):
    return [(i, j) for i in range(count) for j in range(i, count)]


def partner(index, step, count):
    if count & (count - 1) == 0:
        return index ^ step
    return lax.rem(index + count - step, count) if not isinstance(index, int) else (index - step) % count


def target(index, step, count):
    if count & (count - 1) == 0:
        return index ^ step
    return lax.rem(index + step, count) if not isinstance(index, int) else (index + step) % count


def split_kernel(count, keep_ref, got_ref, own_ref, *rest):
    outs, total = rest[:-1], rest[-1]
    total[...] = keep_ref[...] + got_ref[...].astype(F32)
    me = lax.axis_index("grp")
    size = own_ref.shape[0]
    own_ref[...] = total[pl.ds(pl.multiple_of(me * size, 8), size), :]
    for step, out in enumerate(outs, 1):
        to = target(me, step, count)
        out[...] = total[pl.ds(pl.multiple_of(to * size, 8), size), :].astype(out.dtype)


def add_kernel(*refs):
    total = refs[0][...]
    for ref in refs[1:-1]:
        total = total + ref[...].astype(F32)
    refs[-1][...] = total.astype(refs[-1].dtype)


def ordered_kernel(count, own_ref, *rest):
    got, out_ref, table = rest[:-2], rest[-2], rest[-1]
    me = lax.axis_index("dev") // 2
    size = own_ref.shape[0]

    def put(index, value):
        table[pl.ds(pl.multiple_of(index * size, 8), size), :] = value.astype(F32)

    put(me, own_ref[...])
    for step, ref in enumerate(got, 1):
        put(partner(me, step, count), ref[...])
    total = table[pl.ds(0, size), :]
    for i in range(1, count):
        total = total + table[pl.ds(i * size, size), :]
    out_ref[...] = total.astype(out_ref.dtype)


def call(kernel, args, outs, scratch=()):
    return pl.pallas_call(
        kernel,
        in_specs=[VMEM] * len(args),
        out_specs=[VMEM] * len(outs),
        out_shape=[pltpu.VMEM(s, t) for s, t in outs],
        scratch_shapes=[pltpu.VMEM(s, t) for s, t in scratch],
        compiler_params=PARAMS,
    )(*[pltpu.with_memory_space_constraint(x, pltpu.VMEM) for x in args])


def halves(value):
    high = value.astype(BF16)
    return high, (value - high.astype(F32)).astype(BF16)


def dot3(a, b):
    ah, al = halves(a)
    bh, bl = halves(b)
    return dot(jnp.concatenate([ah, ah, al], axis=1), jnp.concatenate([bh, bl, bh], axis=0))


def tdot3(a, b):
    ah, al = halves(a)
    bh, bl = halves(b)
    return contract(
        jnp.concatenate([ah, ah, al], axis=0), jnp.concatenate([bh, bl, bh], axis=0), ((0,), (0,))
    )


PANEL = 8
STRIPE = 40


def eliminate(block, put):
    size = block.shape[0]
    lane = lax.broadcasted_iota(jnp.int32, (1, size), 1)
    cell = lax.broadcasted_iota(jnp.int32, (PANEL, size), 1) - lax.broadcasted_iota(
        jnp.int32, (PANEL, size), 0
    )
    near = min(STRIPE + PANEL, size)
    rows, far = block[:near], block[near:]
    ahead, left, right = None, [], []
    for c in range(0, size, PANEL):
        end = (c // STRIPE + 1) * STRIPE
        wide = [jnp.broadcast_to(rows[:, c + j : c + j + 1], rows.shape) for j in range(PANEL)]
        top = [x[:PANEL] for x in wide] if ahead is None else ahead
        rest = [x[PANEL:] for x in wide]
        last = c + PANEL == size
        here = (lane >= c) & (lane < c + PANEL)
        panel = jnp.where(here, (cell == c).astype(F32), rows[:PANEL])
        if not last:
            below = rows[PANEL:]
            ahead = [
                jnp.broadcast_to(below[:PANEL, at : at + 1], (PANEL, size))
                for at in range(c + PANEL, c + 2 * PANEL)
            ]
            below = jnp.where(here, F32(0.0), below)
        done = []
        for j in range(PANEL):
            scale = lax.rsqrt(top[j][j : j + 1, :])
            row = panel[j : j + 1, :] * scale
            put(c + j, row)
            done.append(row)
            lower = top[j] * scale
            panel = panel - lower * row
            ups = {i: top[i][j : j + 1, :] * scale for i in range(j + 1, PANEL)}
            for i, up in ups.items():
                top[i] = top[i] - lower * up
            if not last:
                lower = rest[j] * scale
                below = below - lower * row
                for i, up in ups.items():
                    rest[i] = rest[i] - lower * up
                lower = lower[:PANEL]
                ahead = [x - lower * lower[i : i + 1, :] for i, x in enumerate(ahead)]
        if last:
            break
        rows = below
        if far.shape[0]:
            done = jnp.concatenate(done, axis=0)
            left.append(done)
            right.append(jnp.where((lane >= c + PANEL) & (lane < end), F32(0.0), done))
            if c + PANEL == end:
                change = tdot3(jnp.concatenate(left, axis=0), jnp.concatenate(right, axis=0))[near:]
                far = jnp.where((lane >= end - STRIPE) & (lane < end), F32(0.0), far) - change
                more = min(end + STRIPE + PANEL, size) - near
                rows = jnp.concatenate([rows, far[:more]], axis=0)
                far, near, left, right = far[more:], near + more, [], []


def factor_kernel(total_rows, groups, tall_ref, *rest):
    mine, other = rest[:groups], rest[groups : 2 * groups]
    basis_hbm, factor_hbm, packed, upper, inverse, basis, sems = rest[2 * groups :]
    me = lax.axis_index("grp")
    core = lax.rem(lax.axis_index("dev"), 2)
    size = mine[0].shape[0]
    for at, refs in ((core, mine), (1 - core, other)):
        for step, ref in enumerate(refs):
            place = at * groups + (partner(me, step, groups) if step else me)
            packed[pl.ds(pl.multiple_of(place * size, 8), size), :] = ref[...]
    columns = tall_ref.shape[1]
    blocks = columns // BLOCK
    span = lambda i: pl.ds(i * BLOCK, BLOCK)
    gram = {
        pair: packed[span(at), :] * F32(1.0 / total_rows) for at, pair in enumerate(triangle(blocks))
    }
    row = lax.broadcasted_iota(jnp.int32, (BLOCK, BLOCK), 0)
    column = lax.broadcasted_iota(jnp.int32, (BLOCK, BLOCK), 1)
    copies = []
    for b in range(blocks):
        here = slice(b * BLOCK, (b + 1) * BLOCK)
        before = slice(0, b * BLOCK)
        last = b + 1 == blocks

        def put(i, value):
            inverse[pl.ds(b * BLOCK + i, 1), here] = value

        mixed = tdot3(upper[before, here], inverse[before, before]) if b else None
        if last and b:
            kept = contract(tall_ref[:, before], mixed.astype(BF16), ((1,), (1,)))
            rest = jnp.concatenate(halves(tall_ref[:, here].astype(F32) - kept), axis=1)
        eliminate(gram[b, b], put)
        diagonal = jnp.where(row >= column, inverse[here, here], F32(0.0))
        strip = {j: dot3(diagonal, gram[b, j]) for j in range(b + 1, blocks)}
        for i in range(b + 1, blocks):
            for j in range(i, blocks):
                gram[i, j] = gram[i, j] - tdot3(strip[i], strip[j])
        for j, value in strip.items():
            upper[here, j * BLOCK : (j + 1) * BLOCK] = value
        if last and b:
            narrow = diagonal.astype(BF16)
            value = contract(rest, jnp.concatenate([narrow, narrow], axis=1), ((1,), (1,)))
        else:
            reach = slice(0, (b + 1) * BLOCK)
            inverse[here, here] = diagonal
            if b:
                inverse[here, before] = -dot3(diagonal, mixed)
            if not last:
                inverse[here, (b + 1) * BLOCK :] = jnp.zeros((BLOCK, columns - (b + 1) * BLOCK), F32)
            value = contract(tall_ref[:, reach], inverse[here, reach].astype(BF16), ((1,), (1,)))
        basis[:, here] = value.astype(BF16)
        copies.append(pltpu.make_async_copy(basis.at[:, here], basis_hbm.at[:, here], sems.at[b]))
        copies[-1].start()
        corner = dot3(diagonal, gram[b, b])
        upper[here, here] = jnp.where(row <= column, corner, F32(0.0))
        if b:
            upper[here, before] = jnp.zeros((BLOCK, b * BLOCK), F32)
    share = factor_hbm.shape[0]
    mine = pl.ds(pl.multiple_of(lax.axis_index("dev") * share, 8), share)
    copies.append(pltpu.make_async_copy(upper.at[mine], factor_hbm, sems.at[blocks]))
    copies[-1].start()
    for copy in copies:
        copy.wait()


def per_device(schur, omega, face_rows):
    matrix, tests, faces = schur[0], omega[0], face_rows[0]
    groups = lax.axis_size("grp")
    devs = lax.axis_size("dev")
    depth = devs // 2
    rows, columns = tests.shape
    inner_size = matrix.shape[1]
    count = faces.shape[1]
    shared = 4 * count

    def flat(pairs):
        return [(g * devs + d, h * devs + e) for g, d, h, e in pairs]

    everywhere = [(g, d) for g in range(groups) for d in range(devs)]
    twin = flat([(g, d, g, d ^ 1) for g, d in everywhere])
    along_dev = flat([(g, d, g, (d + 1 if d % 2 else d - 1) % devs) for g, d in everywhere])
    pair_grp = flat([(g, d, g ^ 1, d) for g, d in everywhere])
    along_grp = flat([(g, d, (g + 1 if g % 2 else g - 1) % groups, d) for g, d in everywhere])
    face_perms = (along_grp, pair_grp, along_dev, twin)

    def swap(values):
        return [lax.ppermute(v, AXES, perm) for v, perm in zip(values, face_perms)]

    face_outs = [((count, columns), BF16)] * 4
    steps = 2 if rows % 256 == 0 else 1
    schur_v, first, gather, faces_v, *sides = pl.pallas_call(
        first_kernel,
        in_specs=[pl.BlockSpec(memory_space=pltpu.HBM)] * 3,
        out_specs=[VMEM] * (4 + len(face_outs)),
        out_shape=[
            pltpu.VMEM(s, t)
            for s, t in [
                ((rows, inner_size), BF16),
                ((rows, columns), BF16),
                ((shared, rows), BF16),
                (faces.shape, jnp.int32),
                *face_outs,
            ]
        ],
        scratch_shapes=[
            pltpu.VMEM((rows, columns), BF16),
            pltpu.SemaphoreType.DMA((2 + steps,)),
        ],
        compiler_params=PARAMS,
    )(*[pltpu.with_memory_space_constraint(x, pltpu.HBM) for x in (matrix, tests, faces)])
    got = swap(sides)
    scatter, whole, face_side, face_whole = call(
        ahead_kernel,
        [schur_v, first, gather, faces_v],
        [
            ((rows, shared), BF16),
            ((rows, columns), F32),
            ((shared, shared), BF16),
            ((shared, columns), F32),
        ],
    )
    received, *sides = call(
        second_faces_kernel, [face_whole, face_side, *got], [((shared, columns), BF16), *face_outs]
    )
    got = swap(sides)

    blocks = columns // BLOCK
    unit = 2 * groups * 8
    packed = -(-len(triangle(blocks)) * BLOCK // unit) * unit
    half = packed // 2
    piece = half // groups
    inner, base = call(
        inner_kernel,
        [schur_v, whole, received, scatter],
        [((rows, columns), BF16), ((packed, BLOCK), F32)],
    )
    outer, keep, send = call(
        gram_kernel,
        [*sides, *got, base],
        [((shared, columns), BF16), ((half, BLOCK), F32), ((half, BLOCK), BF16)],
        [((packed, BLOCK), F32)],
    )
    got = lax.ppermute(send, AXES, twin)
    (tall,) = call(tall_kernel, [inner, outer, scatter], [((rows, columns), BF16)])

    def grp_step(step):
        return flat([(g, d, target(g, step, groups), d) for g, d in everywhere])

    def depth_step(step):
        return flat([(g, d, g, 2 * target(d // 2, step, depth) + d % 2) for g, d in everywhere])

    own, *parts = call(
        functools.partial(split_kernel, groups),
        [keep, got],
        [((piece, BLOCK), F32)] + [((piece, BLOCK), BF16)] * (groups - 1),
        [((half, BLOCK), F32)],
    )
    parts = [lax.ppermute(parts[i - 1], AXES, grp_step(i)) for i in range(groups - 1, 0, -1)]
    (own,) = call(add_kernel, [own, *parts], [((piece, BLOCK), BF16)])
    parts = [lax.ppermute(own, AXES, depth_step(i)) for i in range(1, depth)]
    (own,) = call(
        functools.partial(ordered_kernel, depth),
        [own, *parts],
        [((piece, BLOCK), F32)],
        [((depth * piece, BLOCK), F32)],
    )
    parts = [lax.ppermute(own, AXES, grp_step(i)) for i in range(1, groups)]
    mine = [own, *parts]
    other = [lax.ppermute(v, AXES, twin) for v in mine]
    basis, factor = pl.pallas_call(
        functools.partial(factor_kernel, groups * devs * rows, groups),
        in_specs=[VMEM] * (1 + 2 * groups),
        out_specs=[pl.BlockSpec(memory_space=pl.ANY)] * 2,
        out_shape=[
            jax.ShapeDtypeStruct((rows, columns), BF16),
            jax.ShapeDtypeStruct((columns // devs, columns), F32),
        ],
        scratch_shapes=[
            pltpu.VMEM((packed, BLOCK), F32),
            pltpu.VMEM((columns, columns), F32),
            pltpu.VMEM((columns, columns), F32),
            pltpu.VMEM((rows, columns), BF16),
            pltpu.SemaphoreType.DMA((blocks + 1,)),
        ],
        compiler_params=PARAMS,
    )(*[pltpu.with_memory_space_constraint(x, pltpu.VMEM) for x in (tall, *mine, *other)])
    return basis[None], factor


def solution(mesh):
    return jax.shard_map(
        per_device,
        mesh=mesh,
        in_specs=(P(AXES, None, None),) * 3,
        out_specs=(P(AXES, None, None), P("dev", None)),
        check_vma=False,
    )
```

```python
import functools
import math

import jax
import jax.numpy as jnp
from jax import lax
from jax.experimental import pallas as pl
from jax.experimental.pallas import tpu as pltpu
from jax.sharding import PartitionSpec as P

F32 = jnp.float32
BF16 = jnp.bfloat16
BLOCK = 128
AXES = ("grp", "dev")
VMEM = pl.BlockSpec(memory_space=pltpu.VMEM)
PARAMS = pltpu.CompilerParams(vmem_limit_bytes=20 * 2**20)


def slots_of(face_ref):
    rows = face_ref[...]
    odd_d = lax.rem(lax.axis_index("dev"), 2) == 1
    odd_g = lax.rem(lax.axis_index("grp"), 2) == 1
    f0, f1, f2, f3 = (rows[i : i + 1, :] for i in range(4))
    return (
        jnp.where(odd_g, f3, f2),
        jnp.where(odd_g, f2, f3),
        jnp.where(odd_d, f1, f0),
        jnp.where(odd_d, f0, f1),
    )


def gather_matrix(slots, columns):
    out = []
    for slot in slots:
        count = slot.shape[1]
        column = jnp.transpose(jnp.broadcast_to(slot.astype(F32), (8, count)))[:, 0:1]
        lanes = lax.broadcasted_iota(jnp.int32, (count, columns), 1)
        out.append((column == lanes.astype(F32)).astype(BF16))
    return jnp.concatenate(out, axis=0)


def scatter_matrix(slots, rows):
    out = []
    for slot in slots:
        sub = lax.broadcasted_iota(jnp.int32, (rows, slot.shape[1]), 0)
        out.append((sub == slot).astype(F32).astype(BF16))
    return jnp.concatenate(out, axis=1)


def dot(a, b):
    return jnp.dot(a, b, preferred_element_type=F32)


def contract(a, b, dims, exact=False):
    return lax.dot_general(
        a,
        b,
        (dims, ((), ())),
        precision=lax.Precision.HIGHEST if exact else None,
        preferred_element_type=F32,
    )


def pick(refs):
    return jnp.concatenate([r[...] for r in refs], axis=0)


def spill(value, refs):
    count = refs[0].shape[0]
    for i, ref in enumerate(refs):
        ref[...] = value[i * count : (i + 1) * count].astype(ref.dtype)


def first_kernel(
    schur_hbm, omega_hbm, face_hbm, schur_ref, first_ref, gather, faces, f0, f1, f2, f3, omega, sems
):
    rows = schur_ref.shape[0]
    steps = sems.shape[0] - 2
    chunk = rows // steps
    face_copy = pltpu.make_async_copy(face_hbm, faces, sems.at[0])
    omega_copy = pltpu.make_async_copy(omega_hbm, omega, sems.at[1])
    face_copy.start()
    omega_copy.start()
    copies = []
    for i in range(steps):
        at = pl.ds(i * chunk, chunk)
        copies.append(pltpu.make_async_copy(schur_hbm.at[at], schur_ref.at[at], sems.at[2 + i]))
        copies[-1].start()
    face_copy.wait()
    gather[...] = gather_matrix(slots_of(faces), rows)
    omega_copy.wait()
    for i, copy in enumerate(copies):
        copy.wait()
        at = pl.ds(i * chunk, chunk)
        first_ref[at, :] = dot(schur_ref[at, :], omega[...]).astype(BF16)
    spill(dot(gather[...], first_ref[...]), (f0, f1, f2, f3))


def ahead_kernel(schur_ref, first_ref, gather, faces, scatter, whole, face_side, face_whole):
    scatter[...] = scatter_matrix(slots_of(faces), schur_ref.shape[0])
    face_schur = dot(gather[...], schur_ref[...]).astype(BF16)
    face_whole[...] = dot(face_schur, first_ref[...])
    face_side[...] = dot(face_schur, scatter[...]).astype(BF16)
    whole[...] = dot(schur_ref[...], first_ref[...])


def second_faces_kernel(face_whole, face_side, r0, r1, r2, r3, received, f0, f1, f2, f3):
    received[...] = pick((r0, r1, r2, r3))
    spill(face_whole[...] + dot(face_side[...], received[...]), (f0, f1, f2, f3))


def pack_triangle(packed, value, base=None):
    blocks = value.shape[1] // BLOCK
    side = jnp.transpose(value)
    at = 0
    for i in range(blocks):
        strip = dot(side[i * BLOCK : (i + 1) * BLOCK, :], value[:, i * BLOCK :])
        for j in range(i, blocks):
            part = strip[:, (j - i) * BLOCK : (j - i + 1) * BLOCK]
            here = pl.ds(at * BLOCK, BLOCK)
            packed[here, :] = part if base is None else part + base[here, :]
            at += 1
    spare = packed.shape[0] - at * BLOCK
    if spare:
        packed[pl.ds(at * BLOCK, spare), :] = jnp.zeros((spare, BLOCK), F32)


def inner_kernel(schur_ref, whole, received, scatter, inner, packed):
    shared = dot(scatter[...], jnp.ones((scatter.shape[1], BLOCK), BF16))
    shared = jnp.concatenate([shared] * (whole.shape[1] // BLOCK), axis=1)
    side = dot(schur_ref[...], scatter[...]).astype(BF16)
    second = whole[...] + dot(side, received[...])
    inner[...] = jnp.where(shared > 0.5, F32(0.0), second).astype(BF16)
    pack_triangle(packed, inner[...])


def gram_kernel(f0, f1, f2, f3, r0, r1, r2, r3, base, outer, keep_ref, send_ref, packed):
    total = pick((f0, f1, f2, f3)).astype(F32) + pick((r0, r1, r2, r3)).astype(F32)
    outer[...] = (total * F32(1.0 / math.sqrt(2.0))).astype(BF16)
    pack_triangle(packed, outer[...], base)
    half = keep_ref.shape[0]
    core = lax.rem(lax.axis_index("dev"), 2)
    keep_ref[...] = packed[pl.ds(pl.multiple_of(core * half, 8), half), :]
    send_ref[...] = packed[pl.ds(pl.multiple_of((1 - core) * half, 8), half), :].astype(send_ref.dtype)


def tall_kernel(inner, outer, scatter, tall):
    tall[...] = (inner[...].astype(F32) + dot(scatter[...], outer[...])).astype(BF16)


def triangle(count):
    return [(i, j) for i in range(count) for j in range(i, count)]


def partner(index, step, count):
    if count & (count - 1) == 0:
        return index ^ step
    return lax.rem(index + count - step, count) if not isinstance(index, int) else (index - step) % count


def target(index, step, count):
    if count & (count - 1) == 0:
        return index ^ step
    return lax.rem(index + step, count) if not isinstance(index, int) else (index + step) % count


def split_kernel(count, keep_ref, got_ref, own_ref, *rest):
    outs, total = rest[:-1], rest[-1]
    total[...] = keep_ref[...] + got_ref[...].astype(F32)
    me = lax.axis_index("grp")
    size = own_ref.shape[0]
    own_ref[...] = total[pl.ds(pl.multiple_of(me * size, 8), size), :]
    for step, out in enumerate(outs, 1):
        to = target(me, step, count)
        out[...] = total[pl.ds(pl.multiple_of(to * size, 8), size), :].astype(out.dtype)


def add_kernel(*refs):
    total = refs[0][...]
    for ref in refs[1:-1]:
        total = total + ref[...].astype(F32)
    refs[-1][...] = total.astype(refs[-1].dtype)


def ordered_kernel(count, own_ref, *rest):
    got, out_ref, table = rest[:-2], rest[-2], rest[-1]
    me = lax.axis_index("dev") // 2
    size = own_ref.shape[0]

    def put(index, value):
        table[pl.ds(pl.multiple_of(index * size, 8), size), :] = value.astype(F32)

    put(me, own_ref[...])
    for step, ref in enumerate(got, 1):
        put(partner(me, step, count), ref[...])
    total = table[pl.ds(0, size), :]
    for i in range(1, count):
        total = total + table[pl.ds(i * size, size), :]
    out_ref[...] = total.astype(out_ref.dtype)


def call(kernel, args, outs, scratch=()):
    return pl.pallas_call(
        kernel,
        in_specs=[VMEM] * len(args),
        out_specs=[VMEM] * len(outs),
        out_shape=[pltpu.VMEM(s, t) for s, t in outs],
        scratch_shapes=[pltpu.VMEM(s, t) for s, t in scratch],
        compiler_params=PARAMS,
    )(*[pltpu.with_memory_space_constraint(x, pltpu.VMEM) for x in args])


def halves(value):
    high = value.astype(BF16)
    return high, (value - high.astype(F32)).astype(BF16)


def dot3(a, b):
    ah, al = halves(a)
    bh, bl = halves(b)
    return dot(jnp.concatenate([ah, ah, al], axis=1), jnp.concatenate([bh, bl, bh], axis=0))


def tdot3(a, b):
    ah, al = halves(a)
    bh, bl = halves(b)
    return contract(
        jnp.concatenate([ah, ah, al], axis=0), jnp.concatenate([bh, bl, bh], axis=0), ((0,), (0,))
    )


PANEL = 8
STRIPE = 40


def eliminate(block, put):
    size = block.shape[0]
    lane = lax.broadcasted_iota(jnp.int32, (1, size), 1)
    cell = lax.broadcasted_iota(jnp.int32, (PANEL, size), 1) - lax.broadcasted_iota(
        jnp.int32, (PANEL, size), 0
    )
    near = min(STRIPE + PANEL, size)
    rows, far = block[:near], block[near:]
    ahead, left, right = None, [], []
    for c in range(0, size, PANEL):
        end = (c // STRIPE + 1) * STRIPE
        wide = [jnp.broadcast_to(rows[:, c + j : c + j + 1], rows.shape) for j in range(PANEL)]
        top = [x[:PANEL] for x in wide] if ahead is None else ahead
        rest = [x[PANEL:] for x in wide]
        last = c + PANEL == size
        here = (lane >= c) & (lane < c + PANEL)
        panel = jnp.where(here, (cell == c).astype(F32), rows[:PANEL])
        if not last:
            below = rows[PANEL:]
            ahead = [
                jnp.broadcast_to(below[:PANEL, at : at + 1], (PANEL, size))
                for at in range(c + PANEL, c + 2 * PANEL)
            ]
            below = jnp.where(here, F32(0.0), below)
        done = []
        for j in range(PANEL):
            scale = lax.rsqrt(top[j][j : j + 1, :])
            row = panel[j : j + 1, :] * scale
            put(c + j, row)
            done.append(row)
            lower = top[j] * scale
            panel = panel - lower * row
            ups = {i: top[i][j : j + 1, :] * scale for i in range(j + 1, PANEL)}
            for i, up in ups.items():
                top[i] = top[i] - lower * up
            if not last:
                lower = rest[j] * scale
                below = below - lower * row
                for i, up in ups.items():
                    rest[i] = rest[i] - lower * up
                lower = lower[:PANEL]
                ahead = [x - lower * lower[i : i + 1, :] for i, x in enumerate(ahead)]
        if last:
            break
        rows = below
        if far.shape[0]:
            done = jnp.concatenate(done, axis=0)
            left.append(done)
            right.append(jnp.where((lane >= c + PANEL) & (lane < end), F32(0.0), done))
            if c + PANEL == end:
                change = tdot3(jnp.concatenate(left, axis=0), jnp.concatenate(right, axis=0))[near:]
                far = jnp.where((lane >= end - STRIPE) & (lane < end), F32(0.0), far) - change
                more = min(end + STRIPE + PANEL, size) - near
                rows = jnp.concatenate([rows, far[:more]], axis=0)
                far, near, left, right = far[more:], near + more, [], []


def factor_kernel(total_rows, groups, tall_ref, *rest):
    mine, other = rest[:groups], rest[groups : 2 * groups]
    basis_hbm, factor_hbm, packed, upper, inverse, basis, sems = rest[2 * groups :]
    me = lax.axis_index("grp")
    core = lax.rem(lax.axis_index("dev"), 2)
    size = mine[0].shape[0]
    for at, refs in ((core, mine), (1 - core, other)):
        for step, ref in enumerate(refs):
            place = at * groups + (partner(me, step, groups) if step else me)
            packed[pl.ds(pl.multiple_of(place * size, 8), size), :] = ref[...]
    columns = tall_ref.shape[1]
    blocks = columns // BLOCK
    span = lambda i: pl.ds(i * BLOCK, BLOCK)
    gram = {
        pair: packed[span(at), :] * F32(1.0 / total_rows) for at, pair in enumerate(triangle(blocks))
    }
    row = lax.broadcasted_iota(jnp.int32, (BLOCK, BLOCK), 0)
    column = lax.broadcasted_iota(jnp.int32, (BLOCK, BLOCK), 1)
    copies = []
    for b in range(blocks):
        here = slice(b * BLOCK, (b + 1) * BLOCK)
        before = slice(0, b * BLOCK)
        last = b + 1 == blocks

        def put(i, value):
            inverse[pl.ds(b * BLOCK + i, 1), here] = value

        mixed = tdot3(upper[before, here], inverse[before, before]) if b else None
        if last and b:
            kept = contract(tall_ref[:, before], mixed.astype(BF16), ((1,), (1,)))
            rest = jnp.concatenate(halves(tall_ref[:, here].astype(F32) - kept), axis=1)
        eliminate(gram[b, b], put)
        diagonal = jnp.where(row >= column, inverse[here, here], F32(0.0))
        strip = {j: dot3(diagonal, gram[b, j]) for j in range(b + 1, blocks)}
        for i in range(b + 1, blocks):
            for j in range(i, blocks):
                gram[i, j] = gram[i, j] - tdot3(strip[i], strip[j])
        for j, value in strip.items():
            upper[here, j * BLOCK : (j + 1) * BLOCK] = value
        if last and b:
            narrow = diagonal.astype(BF16)
            value = contract(rest, jnp.concatenate([narrow, narrow], axis=1), ((1,), (1,)))
        else:
            reach = slice(0, (b + 1) * BLOCK)
            inverse[here, here] = diagonal
            if b:
                inverse[here, before] = -dot3(diagonal, mixed)
            if not last:
                inverse[here, (b + 1) * BLOCK :] = jnp.zeros((BLOCK, columns - (b + 1) * BLOCK), F32)
            value = contract(tall_ref[:, reach], inverse[here, reach].astype(BF16), ((1,), (1,)))
        basis[:, here] = value.astype(BF16)
        copies.append(pltpu.make_async_copy(basis.at[:, here], basis_hbm.at[:, here], sems.at[b]))
        copies[-1].start()
        corner = dot3(diagonal, gram[b, b])
        upper[here, here] = jnp.where(row <= column, corner, F32(0.0))
        if b:
            upper[here, before] = jnp.zeros((BLOCK, b * BLOCK), F32)
    share = factor_hbm.shape[0]
    mine = pl.ds(pl.multiple_of(lax.axis_index("dev") * share, 8), share)
    copies.append(pltpu.make_async_copy(upper.at[mine], factor_hbm, sems.at[blocks]))
    copies[-1].start()
    for copy in copies:
        copy.wait()


def per_device(schur, omega, face_rows):
    matrix, tests, faces = schur[0], omega[0], face_rows[0]
    groups = lax.axis_size("grp")
    devs = lax.axis_size("dev")
    depth = devs // 2
    rows, columns = tests.shape
    inner_size = matrix.shape[1]
    count = faces.shape[1]
    shared = 4 * count

    def flat(pairs):
        return [(g * devs + d, h * devs + e) for g, d, h, e in pairs]

    everywhere = [(g, d) for g in range(groups) for d in range(devs)]
    twin = flat([(g, d, g, d ^ 1) for g, d in everywhere])
    along_dev = flat([(g, d, g, (d + 1 if d % 2 else d - 1) % devs) for g, d in everywhere])
    pair_grp = flat([(g, d, g ^ 1, d) for g, d in everywhere])
    along_grp = flat([(g, d, (g + 1 if g % 2 else g - 1) % groups, d) for g, d in everywhere])
    face_perms = (along_grp, pair_grp, along_dev, twin)

    def swap(values):
        return [lax.ppermute(v, AXES, perm) for v, perm in zip(values, face_perms)]

    face_outs = [((count, columns), BF16)] * 4
    steps = 2 if rows % 256 == 0 else 1
    schur_v, first, gather, faces_v, *sides = pl.pallas_call(
        first_kernel,
        in_specs=[pl.BlockSpec(memory_space=pltpu.HBM)] * 3,
        out_specs=[VMEM] * (4 + len(face_outs)),
        out_shape=[
            pltpu.VMEM(s, t)
            for s, t in [
                ((rows, inner_size), BF16),
                ((rows, columns), BF16),
                ((shared, rows), BF16),
                (faces.shape, jnp.int32),
                *face_outs,
            ]
        ],
        scratch_shapes=[
            pltpu.VMEM((rows, columns), BF16),
            pltpu.SemaphoreType.DMA((2 + steps,)),
        ],
        compiler_params=PARAMS,
    )(*[pltpu.with_memory_space_constraint(x, pltpu.HBM) for x in (matrix, tests, faces)])
    got = swap(sides)
    scatter, whole, face_side, face_whole = call(
        ahead_kernel,
        [schur_v, first, gather, faces_v],
        [
            ((rows, shared), BF16),
            ((rows, columns), F32),
            ((shared, shared), BF16),
            ((shared, columns), F32),
        ],
    )
    received, *sides = call(
        second_faces_kernel, [face_whole, face_side, *got], [((shared, columns), BF16), *face_outs]
    )
    got = swap(sides)

    blocks = columns // BLOCK
    unit = 2 * groups * 8
    packed = -(-len(triangle(blocks)) * BLOCK // unit) * unit
    half = packed // 2
    piece = half // groups
    inner, base = call(
        inner_kernel,
        [schur_v, whole, received, scatter],
        [((rows, columns), BF16), ((packed, BLOCK), F32)],
    )
    outer, keep, send = call(
        gram_kernel,
        [*sides, *got, base],
        [((shared, columns), BF16), ((half, BLOCK), F32), ((half, BLOCK), BF16)],
        [((packed, BLOCK), F32)],
    )
    got = lax.ppermute(send, AXES, twin)
    (tall,) = call(tall_kernel, [inner, outer, scatter], [((rows, columns), BF16)])

    def grp_step(step):
        return flat([(g, d, target(g, step, groups), d) for g, d in everywhere])

    def depth_step(step):
        return flat([(g, d, g, 2 * target(d // 2, step, depth) + d % 2) for g, d in everywhere])

    own, *parts = call(
        functools.partial(split_kernel, groups),
        [keep, got],
        [((piece, BLOCK), F32)] + [((piece, BLOCK), BF16)] * (groups - 1),
        [((half, BLOCK), F32)],
    )
    parts = [lax.ppermute(parts[i - 1], AXES, grp_step(i)) for i in range(groups - 1, 0, -1)]
    (own,) = call(add_kernel, [own, *parts], [((piece, BLOCK), BF16)])
    parts = [lax.ppermute(own, AXES, depth_step(i)) for i in range(1, depth)]
    (own,) = call(
        functools.partial(ordered_kernel, depth),
        [own, *parts],
        [((piece, BLOCK), F32)],
        [((depth * piece, BLOCK), F32)],
    )
    parts = [lax.ppermute(own, AXES, grp_step(i)) for i in range(1, groups)]
    mine = [own, *parts]
    other = [lax.ppermute(v, AXES, twin) for v in mine]
    basis, factor = pl.pallas_call(
        functools.partial(factor_kernel, groups * devs * rows, groups),
        in_specs=[VMEM] * (1 + 2 * groups),
        out_specs=[pl.BlockSpec(memory_space=pl.ANY)] * 2,
        out_shape=[
            jax.ShapeDtypeStruct((rows, columns), BF16),
            jax.ShapeDtypeStruct((columns // devs, columns), F32),
        ],
        scratch_shapes=[
            pltpu.VMEM((packed, BLOCK), F32),
            pltpu.VMEM((columns, columns), F32),
            pltpu.VMEM((columns, columns), F32),
            pltpu.VMEM((rows, columns), BF16),
            pltpu.SemaphoreType.DMA((blocks + 1,)),
        ],
        compiler_params=pltpu.CompilerParams(
            vmem_limit_bytes=20 * 2**20
        ),
    )(*[pltpu.with_memory_space_constraint(x, pltpu.VMEM) for x in (tall, *mine, *other)])
    return basis[None], factor


def solution(mesh):
    return jax.shard_map(
        per_device,
        mesh=mesh,
        in_specs=(P(AXES, None, None),) * 3,
        out_specs=(P(AXES, None, None), P("dev", None)),
        check_vma=False,
    )
```
